32 devices in a mesh: grp: 1, seg: 32 (over z, y, x, core).
Axes of the slice: x: 2, y: 2, z: 4, core: 2. Of those that a mesh axis runs over, the one named last changes fastest.
Arguments:
- tokens: bfloat16 [32, 2048, 1024], P(('grp', 'seg')), may hold values from -6 to 6
- cotangent: bfloat16 [32, 2048, 1024], P(('grp', 'seg')), may hold values from -6 to 6
- routing: int32 [32, 64], P(('grp', 'seg')), may hold values from 0 to 15
- w_up: bfloat16 [64, 512, 1024], P(None, 'seg'), may hold values from -1.5 to 1.5
- w_down: bfloat16 [64, 512, 1024], P(None, 'seg'), may hold values from -2 to 2
- momentum_up: float32 [64, 512, 1024], P('grp', 'seg'), may hold values from -24 to 24
- momentum_down: float32 [64, 512, 1024], P('grp', 'seg'), may hold values from -24 to 24
Outputs:
- layer_out: bfloat16 [32, 2048, 1024], P(('grp', 'seg'))
- token_grad: bfloat16 [32, 2048, 1024], P(('grp', 'seg'))
- new_momentum_up: float32 [64, 512, 1024], P('grp', 'seg')
- new_momentum_down: float32 [64, 512, 1024], P('grp', 'seg')
- new_up: bfloat16 [64, 512, 1024], P('grp', 'seg')
- new_down: bfloat16 [64, 512, 1024], P('grp', 'seg')
The draws below stay inside these ranges and needn't reach their ends.
Inputs may be any that keep to these rules, and one draw needn't show every extreme that they name: The routing weight of a segment and expert is this numerator over 512.
All inputs are finite; a program needn't handle non-finite values.
Results may differ from the reference program's by a relative error of at most 0.0075.
Values may be sent and summed in bfloat16 or wider, within the bound.
No kernel may reach another device: no remote copies, remote signals or barrier semaphores. Data moves between devices by JAX's collectives and lax.ppermute only.
A program may use at most 128 MiB of HBM per device.

```python
import jax
import jax.numpy as jnp
from jax import lax

E = 64
D = 1024
H = 512
SEG_LEN = 2048
SEGS = 32


def set_ends(entries, rng, least, high):
    longest = entries.shape.index(max(entries.shape))
    spots = []
    for shift in (0, 1):
        where = [jax.random.randint(jax.random.fold_in(rng, axis), (), 0, length) for axis, length in enumerate(entries.shape)]
        where[longest] = (where[longest] + shift) % entries.shape[longest]
        spots.append(tuple(where))
    return entries.at[spots[0]].set(least).at[spots[1]].set(high)


def block_levels(own_key, extent, shards, low, high):
    def one(dim, blocks):
        draws = jax.random.uniform(jax.random.fold_in(jax.random.fold_in(own_key, 6), dim), (blocks,), jnp.float32, low / len(shards), high / len(shards))
        return jnp.repeat(jnp.exp(draws), extent[dim] // blocks).reshape((-1,) + (1,) * (len(extent) - dim - 1))

    level = one(*shards[0])
    for cut in shards[1:]:
        level = level * one(*cut)
    return level


def scatter_about(rng, extent, scale, reach, cuts=(), held_as=jnp.bfloat16):
    loudness = block_levels(rng, extent, cuts, -0.22, 0.18) if cuts else 1.0
    drawn = jax.random.normal(rng, extent, jnp.float32) * scale * loudness
    return jnp.minimum(jnp.maximum(drawn, -reach), reach).astype(held_as)


def setup_inputs(seed: int = 0) -> dict:
    streams_of = jax.random.split(jax.random.key(seed), 8)
    return {
        "tokens": scatter_about(streams_of[0], (SEGS, SEG_LEN, D), 1.0, 6.0, ((0, 32),)),
        "cotangent": scatter_about(streams_of[1], (SEGS, SEG_LEN, D), 1.0, 6.0, ((0, 32),)),
        "routing": set_ends(jax.random.randint(streams_of[2], (SEGS, E), 0, 16), jax.random.fold_in(streams_of[2], 1), 0, 15).astype(jnp.int32),
        "w_up": scatter_about(streams_of[3], (E, H, D), (D // E) ** -0.5, 1.5, ((1, 32),)),
        "w_down": scatter_about(streams_of[4], (E, H, D), (H // E) ** -0.5, 2.0, ((1, 32),)),
        "momentum_up": scatter_about(streams_of[5], (E, H, D), 4.0, 24.0, ((1, 32),), jnp.float32),
        "momentum_down": scatter_about(streams_of[6], (E, H, D), 4.0, 24.0, ((1, 32),), jnp.float32),
    }


def gelu_parts(pre):
    act = 0.5 * pre * (1.0 + lax.erf(pre * 0.7071067811865476))
    slope = 0.5 * (1.0 + lax.erf(pre * 0.7071067811865476)) + pre * jnp.exp(-0.5 * pre * pre) * 0.3989422804014327
    return act, slope


def reference(tokens, cotangent, routing, w_up, w_down, momentum_up, momentum_down):
    mix = (routing.astype(jnp.float32) / (8.0 * E)).astype(jnp.bfloat16)
    flat_up = w_up.reshape(E, H * D)
    flat_down = w_down.reshape(E, H * D)

    def segment(operands):
        inputs, grads, weights = operands
        up_merged = jnp.dot(weights[None, :], flat_up, preferred_element_type=jnp.float32).astype(jnp.bfloat16).reshape(H, D)
        down_merged = jnp.dot(weights[None, :], flat_down, preferred_element_type=jnp.float32).astype(jnp.bfloat16).reshape(H, D)
        pre = lax.dot_general(inputs, up_merged, (((1,), (1,)), ((), ())), preferred_element_type=jnp.float32)
        act_full, slope = gelu_parts(pre)
        act = act_full.astype(jnp.bfloat16)
        layer_out = jnp.dot(act, down_merged, preferred_element_type=jnp.float32).astype(jnp.bfloat16)
        d_act = lax.dot_general(grads, down_merged, (((1,), (1,)), ((), ())), preferred_element_type=jnp.float32)
        d_pre = (d_act * slope).astype(jnp.bfloat16)
        token_grad = jnp.dot(d_pre, up_merged, preferred_element_type=jnp.float32).astype(jnp.bfloat16)
        grad_up_merged = lax.dot_general(d_pre, inputs, (((0,), (0,)), ((), ())), preferred_element_type=jnp.float32).astype(jnp.bfloat16)
        grad_down_merged = lax.dot_general(act, grads, (((0,), (0,)), ((), ())), preferred_element_type=jnp.float32).astype(jnp.bfloat16)
        return layer_out, token_grad, grad_up_merged.reshape(H * D), grad_down_merged.reshape(H * D)

    layer_out, token_grad, stack_up, stack_down = lax.map(segment, (tokens, cotangent, mix))
    grad_up = lax.dot_general(mix, stack_up, (((0,), (0,)), ((), ())), preferred_element_type=jnp.float32).reshape(E, H, D)
    grad_down = lax.dot_general(mix, stack_down, (((0,), (0,)), ((), ())), preferred_element_type=jnp.float32).reshape(E, H, D)
    new_momentum_up = 0.9 * momentum_up + grad_up
    new_momentum_down = 0.9 * momentum_down + grad_down
    new_up = (w_up.astype(jnp.float32) - 0.01 * new_momentum_up).astype(jnp.bfloat16)
    new_down = (w_down.astype(jnp.float32) - 0.01 * new_momentum_down).astype(jnp.bfloat16)
    return layer_out, token_grad, new_momentum_up, new_momentum_down, new_up, new_down
```

```python
import jax
import jax.numpy as jnp
from jax import lax
from jax.sharding import PartitionSpec as P


def gelu_parts(pre):
    act = 0.5 * pre * (1.0 + lax.erf(pre * 0.7071067811865476))
    slope = (
        0.5 * (1.0 + lax.erf(pre * 0.7071067811865476))
        + pre * jnp.exp(-0.5 * pre * pre) * 0.3989422804014327
    )
    return (act, slope)


def spread(mix, rows):
    segs, experts = mix.shape
    columns = experts * rows
    pick = lax.broadcasted_iota(jnp.int32, (experts, columns), 1) // rows
    pick = pick == lax.broadcasted_iota(jnp.int32, (experts, columns), 0)
    wide = jnp.dot(mix, pick.astype(mix.dtype), preferred_element_type=jnp.float32)
    wide = wide.astype(mix.dtype)[:, None, :]
    shape = (segs, rows, columns)
    same = lax.broadcasted_iota(jnp.int32, shape, 1) == lax.broadcasted_iota(jnp.int32, shape, 2) % rows
    full = jnp.where(same, wide, jnp.zeros((), mix.dtype))
    return full.reshape(segs * rows, columns)


def exchange(blocks):
    return lax.all_to_all(blocks, "seg", split_axis=0, concat_axis=0, tiled=True)


def body(tokens, cotangent, routing, w_up, w_down, momentum_up, momentum_down):
    group_count = lax.axis_size("grp")
    seg_count = lax.axis_size("seg")
    group_index = lax.axis_index("grp")
    experts, slice_rows, width = w_up.shape
    owned = experts // group_count
    hidden = seg_count * slice_rows

    routes = exchange(jnp.broadcast_to(routing[:, None, :], (seg_count, 1, experts)))
    mix = (routes[:, 0].astype(jnp.float32) / (8.0 * experts)).astype(jnp.bfloat16)
    mixer = spread(mix, slice_rows)

    def merged(weights):
        flat = weights.reshape(experts * slice_rows, width)
        sums = jnp.dot(mixer, flat, preferred_element_type=jnp.float32).astype(jnp.bfloat16)
        blocks = exchange(sums.reshape(seg_count, slice_rows, width))
        return blocks.reshape(hidden, width)

    def returned(grads):
        blocks = exchange(grads.astype(jnp.bfloat16).reshape(seg_count, slice_rows, width))
        part = lax.dot_general(
            mixer,
            blocks.reshape(hidden, width),
            (((0,), (0,)), ((), ())),
            preferred_element_type=jnp.float32,
        ).reshape(experts, slice_rows, width)
        if group_count == 1:
            return part
        part = lax.psum_scatter(
            part.astype(jnp.bfloat16), "grp", scatter_dimension=0, tiled=True
        )
        return part.astype(jnp.float32)

    def updated(weights, momentum, grad):
        own = weights
        if group_count > 1:
            own = lax.dynamic_slice_in_dim(weights, group_index * owned, owned, 0)
        new_momentum = 0.9 * momentum + grad
        new = (own.astype(jnp.float32) - 0.01 * new_momentum).astype(jnp.bfloat16)
        return new_momentum, new

    inputs = tokens[0]
    grads = cotangent[0]
    up = merged(w_up)
    down = merged(w_down)
    pre = lax.dot_general(
        inputs, up, (((1,), (1,)), ((), ())), preferred_element_type=jnp.float32
    )
    act_full, slope = gelu_parts(pre)
    act = act_full.astype(jnp.bfloat16)
    grad_down = returned(
        lax.dot_general(act, grads, (((0,), (0,)), ((), ())), preferred_element_type=jnp.float32)
    )
    d_act = lax.dot_general(
        grads, down, (((1,), (1,)), ((), ())), preferred_element_type=jnp.float32
    )
    d_pre = (d_act * slope).astype(jnp.bfloat16)
    grad_up = returned(
        lax.dot_general(d_pre, inputs, (((0,), (0,)), ((), ())), preferred_element_type=jnp.float32)
    )
    layer_out = jnp.dot(act, down, preferred_element_type=jnp.float32).astype(jnp.bfloat16)
    token_grad = jnp.dot(d_pre, up, preferred_element_type=jnp.float32).astype(jnp.bfloat16)
    new_momentum_down, new_down = updated(w_down, momentum_down, grad_down)
    new_momentum_up, new_up = updated(w_up, momentum_up, grad_up)
    return (layer_out[None], token_grad[None], new_momentum_up, new_momentum_down, new_up, new_down)


def solution(mesh):
    in_specs = (
        P(("grp", "seg"), None, None),
        P(("grp", "seg"), None, None),
        P(("grp", "seg"), None),
        P(None, "seg", None),
        P(None, "seg", None),
        P("grp", "seg", None),
        P("grp", "seg", None),
    )
    out_specs = (
        P(("grp", "seg"), None, None),
        P(("grp", "seg"), None, None),
        P("grp", "seg", None),
        P("grp", "seg", None),
        P("grp", "seg", None),
        P("grp", "seg", None),
    )
    return jax.shard_map(body, mesh=mesh, in_specs=in_specs, out_specs=out_specs, check_vma=False)
```

```python
import functools

import jax
import jax.numpy as jnp
from jax import lax
from jax.experimental import pallas as pl
from jax.experimental.pallas import tpu as pltpu
from jax.sharding import PartitionSpec as P


def gelu_parts(pre):
    act = 0.5 * pre * (1.0 + lax.erf(pre * 0.7071067811865476))
    slope = (
        0.5 * (1.0 + lax.erf(pre * 0.7071067811865476))
        + pre * jnp.exp(-0.5 * pre * pre) * 0.3989422804014327
    )
    return (act, slope)


def mix_kernel(rows, route_ref, weight_ref, sum_ref, mixer_ref):
    @pl.when(pl.program_id(0) == 0)
    def _():
        segs, _, experts = route_ref.shape
        columns = experts * rows
        mix = (route_ref[:, 0, :].astype(jnp.float32) / (8.0 * experts)).astype(jnp.bfloat16)
        pick = lax.broadcasted_iota(jnp.int32, (experts, columns), 1) // rows
        pick = pick == lax.broadcasted_iota(jnp.int32, (experts, columns), 0)
        pick = jnp.where(pick, 1.0, 0.0).astype(jnp.bfloat16)
        wide = jnp.dot(mix, pick, preferred_element_type=jnp.float32)
        same = lax.broadcasted_iota(jnp.int32, (rows, columns), 0)
        same = same == lax.broadcasted_iota(jnp.int32, (rows, columns), 1) % rows
        for s in range(segs):
            line = jnp.broadcast_to(wide[s : s + 1, :], (rows, columns))
            mixer_ref[s * rows : (s + 1) * rows, :] = jnp.where(same, line, 0.0).astype(jnp.bfloat16)

    sum_ref[...] = jnp.dot(
        mixer_ref[...], weight_ref[...], preferred_element_type=jnp.float32
    ).astype(jnp.bfloat16)


def mix_first(routes, weights):
    segs = routes.shape[0]
    experts, rows, width = weights.shape
    tile = width // 4
    return pl.pallas_call(
        functools.partial(mix_kernel, rows),
        grid=(width // tile,),
        in_specs=[
            pl.BlockSpec(routes.shape, lambda i: (0, 0, 0)),
            pl.BlockSpec((experts * rows, tile), lambda i: (0, i)),
        ],
        out_specs=[
            pl.BlockSpec((segs * rows, tile), lambda i: (0, i)),
            pl.BlockSpec((segs * rows, experts * rows), lambda i: (0, 0)),
        ],
        out_shape=[
            jax.ShapeDtypeStruct((segs * rows, width), jnp.bfloat16),
            jax.ShapeDtypeStruct((segs * rows, experts * rows), jnp.bfloat16),
        ],
        compiler_params=pltpu.CompilerParams(vmem_limit_bytes=12 << 20),
        name="mix_first",
    )(routes, weights.reshape(experts * rows, width))


def update_kernel(mixer_ref, grad_ref, weight_ref, momentum_ref, new_momentum_ref, new_ref):
    part = jnp.dot(mixer_ref[...], grad_ref[...], preferred_element_type=jnp.float32)
    moved = 0.9 * momentum_ref[...] + part
    new_momentum_ref[...] = moved
    new_ref[...] = (weight_ref[...].astype(jnp.float32) - 0.01 * moved).astype(jnp.bfloat16)


def update(mixer, grads, weights, momentum):
    experts, rows, width = weights.shape
    lines = experts * rows
    tile = lines // 4
    block = pl.BlockSpec((tile, width), lambda i: (i, 0))
    grads = pltpu.with_memory_space_constraint(grads, pltpu.VMEM)
    momentum = pltpu.with_memory_space_constraint(momentum.reshape(lines, width), pltpu.HBM)
    new_momentum, new = pl.pallas_call(
        update_kernel,
        grid=(lines // tile,),
        in_specs=[
            pl.BlockSpec((tile, mixer.shape[1]), lambda i: (i, 0)),
            pl.BlockSpec(memory_space=pltpu.VMEM),
            block,
            block,
        ],
        out_specs=[block, block],
        out_shape=[
            jax.ShapeDtypeStruct((lines, width), jnp.float32),
            jax.ShapeDtypeStruct((lines, width), jnp.bfloat16),
        ],
        compiler_params=pltpu.CompilerParams(vmem_limit_bytes=20 << 20),
        name="update",
    )(mixer, grads, weights.reshape(lines, width), momentum)
    return new_momentum.reshape(weights.shape), new.reshape(weights.shape)


def exchange(blocks):
    return lax.all_to_all(blocks, "seg", split_axis=0, concat_axis=0, tiled=True)


def body(tokens, cotangent, routing, w_up, w_down, momentum_up, momentum_down):
    group_count = lax.axis_size("grp")
    seg_count = lax.axis_size("seg")
    group_index = lax.axis_index("grp")
    experts, slice_rows, width = w_up.shape
    owned = experts // group_count
    hidden = seg_count * slice_rows

    routes = exchange(jnp.broadcast_to(routing[:, None, :], (seg_count, 1, experts)))
    first, mixer = mix_first(routes, w_up)

    def delivered(sums):
        return exchange(sums.reshape(seg_count, slice_rows, width)).reshape(hidden, width)

    def returned(grads):
        return delivered(grads.astype(jnp.bfloat16))

    turned = mixer.T

    def updated(weights, momentum, grads):
        if group_count == 1:
            return update(turned, grads, weights, momentum)
        part = jnp.dot(turned, grads, preferred_element_type=jnp.float32)
        part = part.astype(jnp.bfloat16).reshape(experts, slice_rows, width)
        part = lax.psum_scatter(part, "grp", scatter_dimension=0, tiled=True)
        own = lax.dynamic_slice_in_dim(weights, group_index * owned, owned, 0)
        new_momentum = 0.9 * momentum + part.astype(jnp.float32)
        new = (own.astype(jnp.float32) - 0.01 * new_momentum).astype(jnp.bfloat16)
        return new_momentum, new

    inputs = tokens[0]
    grads = cotangent[0]
    up = delivered(first)
    flat_down = w_down.reshape(experts * slice_rows, width)
    second = jnp.dot(mixer, flat_down, preferred_element_type=jnp.float32)
    down = delivered(second.astype(jnp.bfloat16))
    pre = lax.dot_general(
        inputs, up, (((1,), (1,)), ((), ())), preferred_element_type=jnp.float32
    )
    act_full, slope = gelu_parts(pre)
    act = act_full.astype(jnp.bfloat16)
    grad_down = returned(
        lax.dot_general(act, grads, (((0,), (0,)), ((), ())), preferred_element_type=jnp.float32)
    )
    d_act = lax.dot_general(
        grads, down, (((1,), (1,)), ((), ())), preferred_element_type=jnp.float32
    )
    d_pre = (d_act * slope).astype(jnp.bfloat16)
    grad_up = returned(
        lax.dot_general(d_pre, inputs, (((0,), (0,)), ((), ())), preferred_element_type=jnp.float32)
    )
    new_momentum_down, new_down = updated(w_down, momentum_down, grad_down)
    act, d_pre, new_momentum_down, new_down = lax.optimization_barrier(
        (act, d_pre, new_momentum_down, new_down)
    )
    layer_out = jnp.dot(act, down, preferred_element_type=jnp.float32).astype(jnp.bfloat16)
    token_grad = jnp.dot(d_pre, up, preferred_element_type=jnp.float32).astype(jnp.bfloat16)
    new_momentum_up, new_up = updated(w_up, momentum_up, grad_up)
    return (layer_out[None], token_grad[None], new_momentum_up, new_momentum_down, new_up, new_down)


def solution(mesh):
    in_specs = (
        P(("grp", "seg"), None, None),
        P(("grp", "seg"), None, None),
        P(("grp", "seg"), None),
        P(None, "seg", None),
        P(None, "seg", None),
        P("grp", "seg", None),
        P("grp", "seg", None),
    )
    out_specs = (
        P(("grp", "seg"), None, None),
        P(("grp", "seg"), None, None),
        P("grp", "seg", None),
        P("grp", "seg", None),
        P("grp", "seg", None),
        P("grp", "seg", None),
    )
    return jax.shard_map(body, mesh=mesh, in_specs=in_specs, out_specs=out_specs, check_vma=False)
```

```python
import functools

import jax
import jax.numpy as jnp
from jax import lax
from jax.experimental import pallas as pl
from jax.experimental.pallas import tpu as pltpu
from jax.sharding import PartitionSpec as P

PIECES = 4


def gelu_parts(pre):
    act = 0.5 * pre * (1.0 + lax.erf(pre * 0.7071067811865476))
    slope = (
        0.5 * (1.0 + lax.erf(pre * 0.7071067811865476))
        + pre * jnp.exp(-0.5 * pre * pre) * 0.3989422804014327
    )
    return (act, slope)


def mix_kernel(rows, route_ref, weight_ref, sum_ref, mixer_ref):
    @pl.when(pl.program_id(0) == 0)
    def _():
        segs, _, experts = route_ref.shape
        columns = experts * rows
        mix = (route_ref[:, 0, :].astype(jnp.float32) / (8.0 * experts)).astype(jnp.bfloat16)
        pick = lax.broadcasted_iota(jnp.int32, (experts, columns), 1) // rows
        pick = pick == lax.broadcasted_iota(jnp.int32, (experts, columns), 0)
        pick = jnp.where(pick, 1.0, 0.0).astype(jnp.bfloat16)
        wide = jnp.dot(mix, pick, preferred_element_type=jnp.float32)
        same = lax.broadcasted_iota(jnp.int32, (rows, columns), 0)
        same = same == lax.broadcasted_iota(jnp.int32, (rows, columns), 1) % rows
        for s in range(segs):
            line = jnp.broadcast_to(wide[s : s + 1, :], (rows, columns))
            mixer_ref[s * rows : (s + 1) * rows, :] = jnp.where(same, line, 0.0).astype(jnp.bfloat16)

    tile = sum_ref.shape[1]
    here = pl.ds(pl.multiple_of(pl.program_id(0) * tile, tile), tile)
    sum_ref[...] = jnp.dot(
        mixer_ref[...], weight_ref[:, here], preferred_element_type=jnp.float32
    ).astype(jnp.bfloat16)


def mix_first(routes, weights):
    segs = routes.shape[0]
    experts, rows, width = weights.shape
    tile = width // 4
    return pl.pallas_call(
        functools.partial(mix_kernel, rows),
        grid=(width // tile,),
        in_specs=[
            pl.BlockSpec(routes.shape, lambda i: (0, 0, 0)),
            pl.BlockSpec(memory_space=pltpu.VMEM),
        ],
        out_specs=[
            pl.BlockSpec((segs * rows, tile), lambda i: (0, i)),
            pl.BlockSpec((segs * rows, experts * rows), lambda i: (0, 0)),
        ],
        out_shape=[
            pltpu.HBM((segs * rows, width), jnp.bfloat16),
            jax.ShapeDtypeStruct((segs * rows, experts * rows), jnp.bfloat16),
        ],
        compiler_params=pltpu.CompilerParams(vmem_limit_bytes=12 << 20),
        name="mix_first",
    )(routes, weights.reshape(experts * rows, width))


def fetch_kernel(count, *refs):
    sources, targets, sems = refs[:count], refs[count : 2 * count], refs[2 * count]
    copies = [
        pltpu.make_async_copy(source, target, sems.at[i])
        for i, (source, target) in enumerate(zip(sources, targets))
    ]
    for copy in copies:
        copy.start()
    for copy in copies:
        copy.wait()


def fetch(*arrays):
    count = len(arrays)
    return pl.pallas_call(
        functools.partial(fetch_kernel, count),
        in_specs=[pl.BlockSpec(memory_space=pltpu.HBM)] * count,
        out_specs=[pl.BlockSpec(memory_space=pltpu.VMEM)] * count,
        out_shape=[pltpu.VMEM(array.shape, array.dtype) for array in arrays],
        scratch_shapes=[pltpu.SemaphoreType.DMA((count,))],
        compiler_params=pltpu.CompilerParams(vmem_limit_bytes=1 << 20),
        name="fetch",
    )(*(pltpu.with_memory_space_constraint(array, pltpu.HBM) for array in arrays))


def update_kernel(
    count, mixer_ref, weight_ref, grad_hbm, momentum_hbm, new_momentum_hbm, new_hbm,
    grad_ref, momentum_ref, new_ref, grad_sem, in_sems, out_sems,
):
    lines = momentum_ref.shape[0] // count
    parts = [slice(i * lines, (i + 1) * lines) for i in range(count)]
    first = pltpu.make_async_copy(grad_hbm, grad_ref, grad_sem)
    first.start()
    reads = [
        pltpu.make_async_copy(momentum_hbm.at[here, :], momentum_ref.at[here, :], in_sems.at[i])
        for i, here in enumerate(parts)
    ]
    for read in reads:
        read.start()
    first.wait()
    writes = []
    for i, here in enumerate(parts):
        part = jnp.dot(mixer_ref[here, :], grad_ref[...], preferred_element_type=jnp.float32)
        reads[i].wait()
        moved = 0.9 * momentum_ref[here, :] + part
        momentum_ref[here, :] = moved
        rounded = weight_ref[here, :].astype(jnp.float32) - 0.01 * moved
        new_ref[here, :] = rounded.astype(jnp.bfloat16)
        pairs = ((momentum_ref, new_momentum_hbm), (new_ref, new_hbm))
        for j, (source, target) in enumerate(pairs):
            write = pltpu.make_async_copy(source.at[here, :], target.at[here, :], out_sems.at[i, j])
            write.start()
            writes.append(write)
    for write in writes:
        write.wait()


def update_last(mixer, grads, weights, momentum):
    experts, rows, width = weights.shape
    lines = experts * rows
    count = PIECES if experts % PIECES == 0 else 1
    mixer = pltpu.with_memory_space_constraint(mixer, pltpu.VMEM)
    weights = pltpu.with_memory_space_constraint(weights.reshape(lines, width), pltpu.VMEM)
    momentum = pltpu.with_memory_space_constraint(momentum.reshape(lines, width), pltpu.HBM)
    vmem, hbm = pl.BlockSpec(memory_space=pltpu.VMEM), pl.BlockSpec(memory_space=pltpu.HBM)
    new_momentum, new = pl.pallas_call(
        functools.partial(update_kernel, count),
        in_specs=[vmem, vmem, pl.BlockSpec(memory_space=pl.ANY), hbm],
        out_specs=[hbm, hbm],
        out_shape=[
            jax.ShapeDtypeStruct((lines, width), jnp.float32),
            jax.ShapeDtypeStruct((lines, width), jnp.bfloat16),
        ],
        scratch_shapes=[
            pltpu.VMEM(grads.shape, grads.dtype),
            pltpu.VMEM((lines, width), jnp.float32),
            pltpu.VMEM((lines, width), jnp.bfloat16),
            pltpu.SemaphoreType.DMA,
            pltpu.SemaphoreType.DMA((count,)),
            pltpu.SemaphoreType.DMA((count, 2)),
        ],
        compiler_params=pltpu.CompilerParams(vmem_limit_bytes=12 << 20),
        name="update_last",
    )(mixer, weights, grads, momentum)
    return new_momentum.reshape(experts, rows, width), new.reshape(experts, rows, width)


def exchange(blocks):
    return lax.all_to_all(blocks, "seg", split_axis=0, concat_axis=0, tiled=True)


def body(tokens, cotangent, routing, w_up, w_down, momentum_up, momentum_down):
    group_count = lax.axis_size("grp")
    seg_count = lax.axis_size("seg")
    group_index = lax.axis_index("grp")
    experts, slice_rows, width = w_up.shape
    owned = experts // group_count
    hidden = seg_count * slice_rows

    routes = exchange(jnp.broadcast_to(routing[:, None, :], (seg_count, 1, experts)))
    (early_up,) = fetch(w_up)
    first, mixer = mix_first(routes, early_up)

    def delivered(sums):
        return exchange(sums.reshape(seg_count, slice_rows, width)).reshape(hidden, width)

    def returned(grads):
        return delivered(grads.astype(jnp.bfloat16))

    turned = mixer.T

    def updated(weights, momentum, grads):
        part = jnp.dot(turned, grads, preferred_element_type=jnp.float32)
        part = part.reshape(experts, slice_rows, width)
        if group_count > 1:
            part = part.astype(jnp.bfloat16)
            part = lax.psum_scatter(part, "grp", scatter_dimension=0, tiled=True)
            part = part.astype(jnp.float32)
            weights = lax.dynamic_slice_in_dim(weights, group_index * owned, owned, 0)
        new_momentum = 0.9 * momentum + part
        new = (weights.astype(jnp.float32) - 0.01 * new_momentum).astype(jnp.bfloat16)
        return new_momentum, new

    inputs = tokens[0]
    grads = cotangent[0]
    up = delivered(first)
    flat_down = w_down.reshape(experts * slice_rows, width)
    second = jnp.dot(mixer, flat_down, preferred_element_type=jnp.float32)
    down = delivered(second.astype(jnp.bfloat16))
    pre = lax.dot_general(
        inputs, up, (((1,), (1,)), ((), ())), preferred_element_type=jnp.float32
    )
    act_full, slope = gelu_parts(pre)
    act = act_full.astype(jnp.bfloat16)
    grad_down = returned(
        lax.dot_general(act, grads, (((0,), (0,)), ((), ())), preferred_element_type=jnp.float32)
    )
    d_act = lax.dot_general(
        grads, down, (((1,), (1,)), ((), ())), preferred_element_type=jnp.float32
    )
    d_pre = (d_act * slope).astype(jnp.bfloat16)
    grad_up = returned(
        lax.dot_general(d_pre, inputs, (((0,), (0,)), ((), ())), preferred_element_type=jnp.float32)
    )
    new_momentum_down, new_down = updated(w_down, momentum_down, grad_down)
    act, d_pre, new_momentum_down, new_down = lax.optimization_barrier(
        (act, d_pre, new_momentum_down, new_down)
    )
    layer_out = jnp.dot(act, down, preferred_element_type=jnp.float32).astype(jnp.bfloat16)
    token_grad = jnp.dot(d_pre, up, preferred_element_type=jnp.float32).astype(jnp.bfloat16)
    layer_out, token_grad, late_up = lax.optimization_barrier((layer_out, token_grad, w_up))
    if group_count == 1:
        (late_up,) = fetch(late_up)
        new_momentum_up, new_up = update_last(turned, grad_up, late_up, momentum_up)
    else:
        new_momentum_up, new_up = updated(late_up, momentum_up, grad_up)
    return (layer_out[None], token_grad[None], new_momentum_up, new_momentum_down, new_up, new_down)


def solution(mesh):
    in_specs = (
        P(("grp", "seg"), None, None),
        P(("grp", "seg"), None, None),
        P(("grp", "seg"), None),
        P(None, "seg", None),
        P(None, "seg", None),
        P("grp", "seg", None),
        P("grp", "seg", None),
    )
    out_specs = (
        P(("grp", "seg"), None, None),
        P(("grp", "seg"), None, None),
        P("grp", "seg", None),
        P("grp", "seg", None),
        P("grp", "seg", None),
        P("grp", "seg", None),
    )
    return jax.shard_map(body, mesh=mesh, in_specs=in_specs, out_specs=out_specs, check_vma=False)
```

```python
import functools

import jax
import jax.numpy as jnp
from jax import lax
from jax.experimental import pallas as pl
from jax.experimental.pallas import tpu as pltpu
from jax.sharding import PartitionSpec as P


PIECES = 4
TOP = 4


def gelu_parts(pre):
    act = 0.5 * pre * (1.0 + lax.erf(pre * 0.7071067811865476))
    slope = (
        0.5 * (1.0 + lax.erf(pre * 0.7071067811865476))
        + pre * jnp.exp(-0.5 * pre * pre) * 0.3989422804014327
    )
    return (act, slope)


def mix_of(route_ref):
    experts = route_ref.shape[2]
    return (route_ref[:, 0, :].astype(jnp.float32) / (8.0 * experts)).astype(jnp.bfloat16)


def spread(mix, rows, out_ref):
    lines, columns = mix.shape[0], mix.shape[1] * rows
    pick = lax.broadcasted_iota(jnp.int32, (mix.shape[1], columns), 1) // rows
    pick = pick == lax.broadcasted_iota(jnp.int32, (mix.shape[1], columns), 0)
    pick = jnp.where(pick, 1.0, 0.0).astype(jnp.bfloat16)
    wide = jnp.dot(mix, pick, preferred_element_type=jnp.float32)
    same = lax.broadcasted_iota(jnp.int32, (rows, columns), 0)
    same = same == lax.broadcasted_iota(jnp.int32, (rows, columns), 1) % rows
    for i in range(lines):
        line = jnp.broadcast_to(wide[i : i + 1, :], (rows, columns))
        out_ref[i * rows : (i + 1) * rows, :] = jnp.where(same, line, 0.0).astype(jnp.bfloat16)


def mix_kernel(rows, top, resident, me_ref, route_ref, weight_ref, *refs):
    sum_refs, mixer_ref = refs[:-1], refs[-1]

    @pl.when(pl.program_id(0) == 0)
    def _():
        mix = mix_of(route_ref)
        segs = mix.shape[0]
        if top:
            line = lax.broadcasted_iota(jnp.int32, (segs, segs), 0)
            apart = (line % top) * (segs // top) + line // top
            chosen = lax.broadcasted_iota(jnp.int32, (segs, segs), 1) == (apart ^ me_ref[0])
            chosen = jnp.where(chosen, 1.0, 0.0).astype(jnp.bfloat16)
            mix = jnp.dot(chosen, mix, preferred_element_type=jnp.float32).astype(jnp.bfloat16)
        spread(mix, rows, mixer_ref)

    lines, tile = sum_refs[0].shape
    weight = weight_ref
    if resident:
        here = pl.ds(pl.multiple_of(pl.program_id(0) * tile, tile), tile)
        weight = weight_ref.at[:, here]
    sums = jnp.dot(mixer_ref[...], weight[...], preferred_element_type=jnp.float32)
    for i, sum_ref in enumerate(sum_refs):
        sum_ref[...] = sums[i * lines : (i + 1) * lines, :].astype(jnp.bfloat16)


def mix_call(me, routes, weights, parts, top, resident):
    segs = routes.shape[0]
    experts, rows, width = weights.shape
    tile = width // 4
    lines = segs * rows // parts
    weights = weights.reshape(experts * rows, width)
    whole = pl.BlockSpec(memory_space=pltpu.VMEM)
    if not resident:
        weights = pltpu.with_memory_space_constraint(weights, pltpu.HBM)
    return pl.pallas_call(
        functools.partial(mix_kernel, rows, top, resident),
        grid=(width // tile,),
        in_specs=[
            pl.BlockSpec(memory_space=pltpu.SMEM),
            pl.BlockSpec(routes.shape, lambda i: (0, 0, 0)),
            whole if resident else pl.BlockSpec((experts * rows, tile), lambda i: (0, i)),
        ],
        out_specs=[pl.BlockSpec((lines, tile), lambda i: (0, i))] * parts,
        out_shape=[pltpu.HBM((lines, width), jnp.bfloat16)] * parts,
        scratch_shapes=[pltpu.VMEM((segs * rows, experts * rows), jnp.bfloat16)],
        compiler_params=pltpu.CompilerParams(vmem_limit_bytes=12 << 20),
        name="mix",
    )(me, routes, weights)


def turn_kernel(rows, route_ref, out_ref):
    spread(mix_of(route_ref).astype(jnp.float32).T.astype(jnp.bfloat16), rows, out_ref)


def turn(routes, rows):
    segs, _, experts = routes.shape
    return pl.pallas_call(
        functools.partial(turn_kernel, rows),
        out_shape=jax.ShapeDtypeStruct((experts * rows, segs * rows), jnp.bfloat16),
        compiler_params=pltpu.CompilerParams(vmem_limit_bytes=8 << 20),
        name="turn",
    )(routes)


def in_hbm(*arrays):
    return [pltpu.with_memory_space_constraint(array, pltpu.HBM) for array in arrays]


def copy_all(copies):
    for copy in copies:
        copy.start()
    for copy in copies:
        copy.wait()


def regroup_kernel(low, top, rows, *refs):
    plane, send, sems = refs[:low], refs[low : low + top - 1], refs[low + top - 1]
    copy_all(
        [
            pltpu.make_async_copy(
                plane[k].at[pl.ds(z * rows, rows), :],
                send[z - 1].at[pl.ds(k * rows, rows), :],
                sems.at[k, z - 1],
            )
            for z in range(1, top)
            for k in range(low)
        ]
    )


def settle_kernel(low, top, rows, me_ref, *refs):
    plane, got, out_ref, sems = refs[:low], refs[low : low + top - 1], refs[-2], refs[-1]
    copies = []
    for z in range(top):
        for k in range(low):
            source = plane[k].at[pl.ds(0, rows), :]
            if z:
                source = got[z - 1].at[pl.ds(k * rows, rows), :]
            place = pl.multiple_of((me_ref[0] ^ (z * low + k)) * rows, rows)
            copies.append(
                pltpu.make_async_copy(source, out_ref.at[pl.ds(place, rows), :], sems.at[k, z])
            )
    copy_all(copies)


def by_permutes(me, parts, segs, rows, top):
    low = segs // top
    width = parts[0].shape[1]
    hbm, free = pl.BlockSpec(memory_space=pltpu.HBM), pl.BlockSpec(memory_space=pl.ANY)

    def swap(block, apart):
        return lax.ppermute(block, "seg", [(i, i ^ apart) for i in range(segs)])

    plane = [parts[0]] + [swap(parts[k], k) for k in range(1, low)]
    send = pl.pallas_call(
        functools.partial(regroup_kernel, low, top, rows),
        in_specs=[hbm] + [free] * (low - 1),
        out_specs=[hbm] * (top - 1),
        out_shape=[pltpu.HBM((low * rows, width), jnp.bfloat16)] * (top - 1),
        scratch_shapes=[pltpu.SemaphoreType.DMA((low, top - 1))],
        compiler_params=pltpu.CompilerParams(vmem_limit_bytes=1 << 20),
        name="regroup",
    )(*in_hbm(plane[0]), *plane[1:])
    got = [swap(send[z - 1], z * low) for z in range(1, top)]
    return pl.pallas_call(
        functools.partial(settle_kernel, low, top, rows),
        in_specs=[pl.BlockSpec(memory_space=pltpu.SMEM), hbm] + [free] * (low + top - 2),
        out_specs=hbm,
        out_shape=pltpu.HBM((segs * rows, width), jnp.bfloat16),
        scratch_shapes=[pltpu.SemaphoreType.DMA((low, top))],
        compiler_params=pltpu.CompilerParams(vmem_limit_bytes=1 << 20),
        name="settle",
    )(me, *in_hbm(plane[0]), *plane[1:], *got)


def fetch_kernel(count, *refs):
    sources, targets, sems = refs[:count], refs[count : 2 * count], refs[2 * count]
    copies = [
        pltpu.make_async_copy(source, target, sems.at[i])
        for i, (source, target) in enumerate(zip(sources, targets))
    ]
    for copy in copies:
        copy.start()
    for copy in copies:
        copy.wait()


def fetch(*arrays):
    count = len(arrays)
    return pl.pallas_call(
        functools.partial(fetch_kernel, count),
        in_specs=[pl.BlockSpec(memory_space=pltpu.HBM)] * count,
        out_specs=[pl.BlockSpec(memory_space=pltpu.VMEM)] * count,
        out_shape=[pltpu.VMEM(array.shape, array.dtype) for array in arrays],
        scratch_shapes=[pltpu.SemaphoreType.DMA((count,))],
        compiler_params=pltpu.CompilerParams(vmem_limit_bytes=1 << 20),
        name="fetch",
    )(*(pltpu.with_memory_space_constraint(array, pltpu.HBM) for array in arrays))


def update_kernel(
    count, mixer_ref, weight_ref, grad_hbm, momentum_hbm, new_momentum_hbm, new_hbm,
    grad_ref, momentum_ref, new_ref, grad_sem, in_sems, out_sems,
):
    lines = momentum_ref.shape[0] // count
    parts = [slice(i * lines, (i + 1) * lines) for i in range(count)]
    first = pltpu.make_async_copy(grad_hbm, grad_ref, grad_sem)
    first.start()
    reads = [
        pltpu.make_async_copy(momentum_hbm.at[here, :], momentum_ref.at[here, :], in_sems.at[i])
        for i, here in enumerate(parts)
    ]
    for read in reads:
        read.start()
    first.wait()
    writes = []
    for i, here in enumerate(parts):
        part = jnp.dot(mixer_ref[here, :], grad_ref[...], preferred_element_type=jnp.float32)
        reads[i].wait()
        moved = 0.9 * momentum_ref[here, :] + part
        momentum_ref[here, :] = moved
        rounded = weight_ref[here, :].astype(jnp.float32) - 0.01 * moved
        new_ref[here, :] = rounded.astype(jnp.bfloat16)
        pairs = ((momentum_ref, new_momentum_hbm), (new_ref, new_hbm))
        for j, (source, target) in enumerate(pairs):
            write = pltpu.make_async_copy(source.at[here, :], target.at[here, :], out_sems.at[i, j])
            write.start()
            writes.append(write)
    for write in writes:
        write.wait()


def update_last(mixer, grads, weights, momentum):
    experts, rows, width = weights.shape
    lines = experts * rows
    count = PIECES if experts % PIECES == 0 else 1
    mixer = pltpu.with_memory_space_constraint(mixer, pltpu.VMEM)
    weights = pltpu.with_memory_space_constraint(weights.reshape(lines, width), pltpu.VMEM)
    momentum = pltpu.with_memory_space_constraint(momentum.reshape(lines, width), pltpu.HBM)
    vmem, hbm = pl.BlockSpec(memory_space=pltpu.VMEM), pl.BlockSpec(memory_space=pltpu.HBM)
    new_momentum, new = pl.pallas_call(
        functools.partial(update_kernel, count),
        in_specs=[vmem, vmem, pl.BlockSpec(memory_space=pl.ANY), hbm],
        out_specs=[hbm, hbm],
        out_shape=[
            jax.ShapeDtypeStruct((lines, width), jnp.float32),
            jax.ShapeDtypeStruct((lines, width), jnp.bfloat16),
        ],
        scratch_shapes=[
            pltpu.VMEM(grads.shape, grads.dtype),
            pltpu.VMEM((lines, width), jnp.float32),
            pltpu.VMEM((lines, width), jnp.bfloat16),
            pltpu.SemaphoreType.DMA,
            pltpu.SemaphoreType.DMA((count,)),
            pltpu.SemaphoreType.DMA((count, 2)),
        ],
        compiler_params=pltpu.CompilerParams(vmem_limit_bytes=12 << 20),
        name="update_last",
    )(mixer, weights, grads, momentum)
    return new_momentum.reshape(experts, rows, width), new.reshape(experts, rows, width)


def exchange(blocks):
    return lax.all_to_all(blocks, "seg", split_axis=0, concat_axis=0, tiled=True)


def step(tokens, cotangent, routing, w_up, w_down, momentum_up, momentum_down):
    group_count = lax.axis_size("grp")
    seg_count = lax.axis_size("seg")
    group_index = lax.axis_index("grp")
    experts, slice_rows, width = w_up.shape
    owned = experts // group_count
    hidden = seg_count * slice_rows

    routes = exchange(jnp.broadcast_to(routing[:, None, :], (seg_count, 1, experts)))
    me = lax.axis_index("seg").astype(jnp.int32)[None]
    (early_up,) = fetch(w_up)
    first = mix_call(me, routes, early_up, 1, 0, True)[0]

    def delivered(sums):
        return exchange(sums.reshape(seg_count, slice_rows, width)).reshape(hidden, width)

    def returned(grads):
        return delivered(grads.astype(jnp.bfloat16))

    turned = turn(routes, slice_rows)

    def updated(weights, momentum, grads):
        part = jnp.dot(turned, grads, preferred_element_type=jnp.float32)
        part = part.reshape(experts, slice_rows, width)
        if group_count > 1:
            part = part.astype(jnp.bfloat16)
            part = lax.psum_scatter(part, "grp", scatter_dimension=0, tiled=True)
            part = part.astype(jnp.float32)
            weights = lax.dynamic_slice_in_dim(weights, group_index * owned, owned, 0)
        new_momentum = 0.9 * momentum + part
        new = (weights.astype(jnp.float32) - 0.01 * new_momentum).astype(jnp.bfloat16)
        return new_momentum, new

    inputs = tokens[0]
    grads = cotangent[0]
    up = delivered(first)
    top = TOP if seg_count % TOP == 0 and seg_count & (seg_count - 1) == 0 else 0
    if top:
        parts = mix_call(me, routes, w_down, seg_count // top, top, False)
        down = by_permutes(me, parts, seg_count, slice_rows, top)
    else:
        down = delivered(mix_call(me, routes, w_down, 1, 0, False)[0])
    pre = lax.dot_general(inputs, up, (((1,), (1,)), ((), ())), preferred_element_type=jnp.float32)
    act_full, slope = gelu_parts(pre)
    act = act_full.astype(jnp.bfloat16)
    grad_down = returned(
        lax.dot_general(act, grads, (((0,), (0,)), ((), ())), preferred_element_type=jnp.float32),
    )
    d_act = lax.dot_general(
        grads, down, (((1,), (1,)), ((), ())), preferred_element_type=jnp.float32
    )
    d_pre = (d_act * slope).astype(jnp.bfloat16)
    grad_up = returned(
        lax.dot_general(d_pre, inputs, (((0,), (0,)), ((), ())), preferred_element_type=jnp.float32),
    )
    new_momentum_down, new_down = updated(w_down, momentum_down, grad_down)
    act, d_pre, new_momentum_down, new_down = lax.optimization_barrier(
        (act, d_pre, new_momentum_down, new_down)
    )
    layer_out = jnp.dot(act, down, preferred_element_type=jnp.float32).astype(jnp.bfloat16)
    token_grad = jnp.dot(d_pre, up, preferred_element_type=jnp.float32).astype(jnp.bfloat16)
    layer_out, token_grad, late_up = lax.optimization_barrier((layer_out, token_grad, w_up))
    if group_count == 1:
        (late_up,) = fetch(late_up)
        new_momentum_up, new_up = update_last(turned, grad_up, late_up, momentum_up)
    else:
        new_momentum_up, new_up = updated(late_up, momentum_up, grad_up)
    return (layer_out[None], token_grad[None], new_momentum_up, new_momentum_down, new_up, new_down)


def solution(mesh):
    in_specs = (
        P(("grp", "seg"), None, None),
        P(("grp", "seg"), None, None),
        P(("grp", "seg"), None),
        P(None, "seg", None),
        P(None, "seg", None),
        P("grp", "seg", None),
        P("grp", "seg", None),
    )
    out_specs = (
        P(("grp", "seg"), None, None),
        P(("grp", "seg"), None, None),
        P("grp", "seg", None),
        P("grp", "seg", None),
        P("grp", "seg", None),
        P("grp", "seg", None),
    )
    return jax.shard_map(step, mesh=mesh, in_specs=in_specs, out_specs=out_specs, check_vma=False)
```

```python
import functools

import jax
import jax.numpy as jnp
from jax import lax
from jax.experimental import pallas as pl
from jax.experimental.pallas import tpu as pltpu
from jax.sharding import PartitionSpec as P


PIECES = 4
TOP = 8


def gelu_parts(pre):
    act = 0.5 * pre * (1.0 + lax.erf(pre * 0.7071067811865476))
    slope = (
        0.5 * (1.0 + lax.erf(pre * 0.7071067811865476))
        + pre * jnp.exp(-0.5 * pre * pre) * 0.3989422804014327
    )
    return (act, slope)


def mix_of(route_ref):
    experts = route_ref.shape[2]
    return (route_ref[:, 0, :].astype(jnp.float32) / (8.0 * experts)).astype(jnp.bfloat16)


def spread(mix, rows, out_ref):
    lines, columns = mix.shape[0], mix.shape[1] * rows
    pick = lax.broadcasted_iota(jnp.int32, (mix.shape[1], columns), 1) // rows
    pick = pick == lax.broadcasted_iota(jnp.int32, (mix.shape[1], columns), 0)
    pick = jnp.where(pick, 1.0, 0.0).astype(jnp.bfloat16)
    wide = jnp.dot(mix, pick, preferred_element_type=jnp.float32)
    same = lax.broadcasted_iota(jnp.int32, (rows, columns), 0)
    same = same == lax.broadcasted_iota(jnp.int32, (rows, columns), 1) % rows
    for i in range(lines):
        line = jnp.broadcast_to(wide[i : i + 1, :], (rows, columns))
        out_ref[i * rows : (i + 1) * rows, :] = jnp.where(same, line, 0.0).astype(jnp.bfloat16)


def mix_kernel(rows, top, resident, me_ref, route_ref, weight_ref, *refs):
    sum_refs, mixer_ref = refs[:-1], refs[-1]

    @pl.when(pl.program_id(0) == 0)
    def _():
        mix = mix_of(route_ref)
        segs = mix.shape[0]
        if top:
            line = lax.broadcasted_iota(jnp.int32, (segs, segs), 0)
            apart = (line % top) * (segs // top) + line // top
            chosen = lax.broadcasted_iota(jnp.int32, (segs, segs), 1) == (apart ^ me_ref[0])
            chosen = jnp.where(chosen, 1.0, 0.0).astype(jnp.bfloat16)
            mix = jnp.dot(chosen, mix, preferred_element_type=jnp.float32).astype(jnp.bfloat16)
        spread(mix, rows, mixer_ref)

    lines, tile = sum_refs[0].shape
    weight = weight_ref
    if resident:
        here = pl.ds(pl.multiple_of(pl.program_id(0) * tile, tile), tile)
        weight = weight_ref.at[:, here]
    sums = jnp.dot(mixer_ref[...], weight[...], preferred_element_type=jnp.float32)
    for i, sum_ref in enumerate(sum_refs):
        sum_ref[...] = sums[i * lines : (i + 1) * lines, :].astype(jnp.bfloat16)


def mix_call(me, routes, weights, parts, top, resident):
    segs = routes.shape[0]
    experts, rows, width = weights.shape
    tile = width // 4
    lines = segs * rows // parts
    weights = weights.reshape(experts * rows, width)
    whole = pl.BlockSpec(memory_space=pltpu.VMEM)
    if not resident:
        weights = pltpu.with_memory_space_constraint(weights, pltpu.HBM)
    return pl.pallas_call(
        functools.partial(mix_kernel, rows, top, resident),
        grid=(width // tile,),
        in_specs=[
            pl.BlockSpec(memory_space=pltpu.SMEM),
            pl.BlockSpec(routes.shape, lambda i: (0, 0, 0)),
            whole if resident else pl.BlockSpec((experts * rows, tile), lambda i: (0, i)),
        ],
        out_specs=[pl.BlockSpec((lines, tile), lambda i: (0, i))] * parts,
        out_shape=[pltpu.HBM((lines, width), jnp.bfloat16)] * parts,
        scratch_shapes=[pltpu.VMEM((segs * rows, experts * rows), jnp.bfloat16)],
        compiler_params=pltpu.CompilerParams(vmem_limit_bytes=12 << 20),
        name="mix",
    )(me, routes, weights)


def turn_kernel(rows, route_ref, out_ref):
    spread(mix_of(route_ref).astype(jnp.float32).T.astype(jnp.bfloat16), rows, out_ref)


def turn(routes, rows):
    segs, _, experts = routes.shape
    return pl.pallas_call(
        functools.partial(turn_kernel, rows),
        out_shape=jax.ShapeDtypeStruct((experts * rows, segs * rows), jnp.bfloat16),
        compiler_params=pltpu.CompilerParams(vmem_limit_bytes=8 << 20),
        name="turn",
    )(routes)


def in_hbm(*arrays):
    return [pltpu.with_memory_space_constraint(array, pltpu.HBM) for array in arrays]


def copy_all(copies):
    for copy in copies:
        copy.start()
    for copy in copies:
        copy.wait()


def regroup_kernel(low, top, rows, *refs):
    plane, send = refs[:low], refs[low:]
    for z in range(1, top):
        for k in range(low):
            send[z - 1][k * rows : (k + 1) * rows, :] = plane[k][z * rows : (z + 1) * rows, :]


def settle_kernel(low, top, rows, me_ref, *refs):
    plane, got, out_ref, sems = refs[:low], refs[low : low + top - 1], refs[-2], refs[-1]
    copies = []
    for z in range(top):
        for k in range(low):
            source = plane[k].at[pl.ds(0, rows), :]
            if z:
                source = got[z - 1].at[pl.ds(k * rows, rows), :]
            place = pl.multiple_of((me_ref[0] ^ (z * low + k)) * rows, rows)
            copies.append(
                pltpu.make_async_copy(source, out_ref.at[pl.ds(place, rows), :], sems.at[k, z])
            )
    copy_all(copies)


def by_permutes(me, parts, segs, rows, top):
    low = segs // top
    width = parts[0].shape[1]
    hbm, free = pl.BlockSpec(memory_space=pltpu.HBM), pl.BlockSpec(memory_space=pl.ANY)
    near = pl.BlockSpec(memory_space=pltpu.VMEM)

    def swap(block, apart):
        return lax.ppermute(block, "seg", [(i, i ^ apart) for i in range(segs)])

    plane = [parts[0]] + [swap(parts[k], k) for k in range(1, low)]
    send = pl.pallas_call(
        functools.partial(regroup_kernel, low, top, rows),
        in_specs=[near] * low,
        out_specs=[near] * (top - 1),
        out_shape=[pltpu.VMEM((low * rows, width), jnp.bfloat16)] * (top - 1),
        compiler_params=pltpu.CompilerParams(vmem_limit_bytes=4 << 20),
        name="regroup",
    )(*plane)
    got = [swap(send[z - 1], z * low) for z in reversed(range(1, top))][::-1]
    return pl.pallas_call(
        functools.partial(settle_kernel, low, top, rows),
        in_specs=[pl.BlockSpec(memory_space=pltpu.SMEM), hbm] + [free] * (low + top - 2),
        out_specs=hbm,
        out_shape=pltpu.HBM((segs * rows, width), jnp.bfloat16),
        scratch_shapes=[pltpu.SemaphoreType.DMA((low, top))],
        compiler_params=pltpu.CompilerParams(vmem_limit_bytes=1 << 20),
        name="settle",
    )(me, *in_hbm(plane[0]), *plane[1:], *got)


def fetch_kernel(count, *refs):
    sources, targets, sems = refs[:count], refs[count : 2 * count], refs[2 * count]
    copies = [
        pltpu.make_async_copy(source, target, sems.at[i])
        for i, (source, target) in enumerate(zip(sources, targets))
    ]
    for copy in copies:
        copy.start()
    for copy in copies:
        copy.wait()


def fetch(*arrays):
    count = len(arrays)
    return pl.pallas_call(
        functools.partial(fetch_kernel, count),
        in_specs=[pl.BlockSpec(memory_space=pltpu.HBM)] * count,
        out_specs=[pl.BlockSpec(memory_space=pltpu.VMEM)] * count,
        out_shape=[pltpu.VMEM(array.shape, array.dtype) for array in arrays],
        scratch_shapes=[pltpu.SemaphoreType.DMA((count,))],
        compiler_params=pltpu.CompilerParams(vmem_limit_bytes=1 << 20),
        name="fetch",
    )(*(pltpu.with_memory_space_constraint(array, pltpu.HBM) for array in arrays))


def update_kernel(
    count, rows, route_ref, grad_ref, weight_ref, momentum_hbm, new_momentum_hbm, new_hbm,
    mixer_ref, momentum_ref, new_ref, in_sems, out_sems,
):
    lines = momentum_ref.shape[0] // count
    parts = [slice(i * lines, (i + 1) * lines) for i in range(count)]
    reads = [
        pltpu.make_async_copy(momentum_hbm.at[here, :], momentum_ref.at[here, :], in_sems.at[i])
        for i, here in enumerate(parts)
    ]
    for read in reads:
        read.start()
    turn_kernel(rows, route_ref, mixer_ref)
    writes = []
    for i, here in enumerate(parts):
        part = jnp.dot(mixer_ref[here, :], grad_ref[...], preferred_element_type=jnp.float32)
        reads[i].wait()
        moved = 0.9 * momentum_ref[here, :] + part
        momentum_ref[here, :] = moved
        rounded = weight_ref[here, :].astype(jnp.float32) - 0.01 * moved
        new_ref[here, :] = rounded.astype(jnp.bfloat16)
        pairs = ((momentum_ref, new_momentum_hbm), (new_ref, new_hbm))
        for j, (source, target) in enumerate(pairs):
            write = pltpu.make_async_copy(source.at[here, :], target.at[here, :], out_sems.at[i, j])
            write.start()
            writes.append(write)
    for write in writes:
        write.wait()


def update_last(routes, grads, weights, momentum):
    experts, rows, width = weights.shape
    lines = experts * rows
    count = PIECES if experts % PIECES == 0 else 1
    weights = pltpu.with_memory_space_constraint(weights.reshape(lines, width), pltpu.VMEM)
    grads = pltpu.with_memory_space_constraint(grads, pltpu.VMEM)
    momentum = pltpu.with_memory_space_constraint(momentum.reshape(lines, width), pltpu.HBM)
    vmem, hbm = pl.BlockSpec(memory_space=pltpu.VMEM), pl.BlockSpec(memory_space=pltpu.HBM)
    new_momentum, new = pl.pallas_call(
        functools.partial(update_kernel, count, rows),
        in_specs=[vmem, vmem, vmem, hbm],
        out_specs=[hbm, hbm],
        out_shape=[
            jax.ShapeDtypeStruct((lines, width), jnp.float32),
            jax.ShapeDtypeStruct((lines, width), jnp.bfloat16),
        ],
        scratch_shapes=[
            pltpu.VMEM((lines, grads.shape[0]), jnp.bfloat16),
            pltpu.VMEM((lines, width), jnp.float32),
            pltpu.VMEM((lines, width), jnp.bfloat16),
            pltpu.SemaphoreType.DMA((count,)),
            pltpu.SemaphoreType.DMA((count, 2)),
        ],
        compiler_params=pltpu.CompilerParams(vmem_limit_bytes=14 << 20),
        name="update_last",
    )(routes, grads, weights, momentum)
    return new_momentum.reshape(experts, rows, width), new.reshape(experts, rows, width)


def exchange(blocks):
    return lax.all_to_all(blocks, "seg", split_axis=0, concat_axis=0, tiled=True)


def step(tokens, cotangent, routing, w_up, w_down, momentum_up, momentum_down):
    group_count = lax.axis_size("grp")
    seg_count = lax.axis_size("seg")
    group_index = lax.axis_index("grp")
    experts, slice_rows, width = w_up.shape
    owned = experts // group_count
    hidden = seg_count * slice_rows

    routes = exchange(jnp.broadcast_to(routing[:, None, :], (seg_count, 1, experts)))
    me = lax.axis_index("seg").astype(jnp.int32)[None]
    (early_up,) = fetch(w_up)
    first = mix_call(me, routes, early_up, 1, 0, True)[0]

    def delivered(sums):
        return exchange(sums.reshape(seg_count, slice_rows, width)).reshape(hidden, width)

    def returned(grads):
        return delivered(grads.astype(jnp.bfloat16))

    turned = turn(routes, slice_rows)

    def updated(weights, momentum, grads):
        part = jnp.dot(turned, grads, preferred_element_type=jnp.float32)
        part = part.reshape(experts, slice_rows, width)
        if group_count > 1:
            part = part.astype(jnp.bfloat16)
            part = lax.psum_scatter(part, "grp", scatter_dimension=0, tiled=True)
            part = part.astype(jnp.float32)
            weights = lax.dynamic_slice_in_dim(weights, group_index * owned, owned, 0)
        new_momentum = 0.9 * momentum + part
        new = (weights.astype(jnp.float32) - 0.01 * new_momentum).astype(jnp.bfloat16)
        return new_momentum, new

    inputs = tokens[0]
    grads = cotangent[0]
    up = delivered(first)
    top = TOP if seg_count % TOP == 0 and seg_count & (seg_count - 1) == 0 else 0
    if top:
        parts = mix_call(me, routes, w_down, seg_count // top, top, False)
        down = by_permutes(me, parts, seg_count, slice_rows, top)
    else:
        down = delivered(mix_call(me, routes, w_down, 1, 0, False)[0])
    pre = lax.dot_general(inputs, up, (((1,), (1,)), ((), ())), preferred_element_type=jnp.float32)
    act_full, slope = gelu_parts(pre)
    act = act_full.astype(jnp.bfloat16)
    grad_down = returned(
        lax.dot_general(act, grads, (((0,), (0,)), ((), ())), preferred_element_type=jnp.float32),
    )
    d_act = lax.dot_general(
        grads, down, (((1,), (1,)), ((), ())), preferred_element_type=jnp.float32
    )
    d_pre = (d_act * slope).astype(jnp.bfloat16)
    grad_up = returned(
        lax.dot_general(d_pre, inputs, (((0,), (0,)), ((), ())), preferred_element_type=jnp.float32),
    )
    new_momentum_down, new_down = updated(w_down, momentum_down, grad_down)
    act, d_pre, new_momentum_down, new_down = lax.optimization_barrier(
        (act, d_pre, new_momentum_down, new_down)
    )
    layer_out = jnp.dot(act, down, preferred_element_type=jnp.float32).astype(jnp.bfloat16)
    token_grad = jnp.dot(d_pre, up, preferred_element_type=jnp.float32).astype(jnp.bfloat16)
    layer_out, token_grad, late_up = lax.optimization_barrier((layer_out, token_grad, w_up))
    if group_count == 1:
        (late_up,) = fetch(late_up)
        new_momentum_up, new_up = update_last(routes, grad_up, late_up, momentum_up)
    else:
        new_momentum_up, new_up = updated(late_up, momentum_up, grad_up)
    return (layer_out[None], token_grad[None], new_momentum_up, new_momentum_down, new_up, new_down)


def solution(mesh):
    in_specs = (
        P(("grp", "seg"), None, None),
        P(("grp", "seg"), None, None),
        P(("grp", "seg"), None),
        P(None, "seg", None),
        P(None, "seg", None),
        P("grp", "seg", None),
        P("grp", "seg", None),
    )
    out_specs = (
        P(("grp", "seg"), None, None),
        P(("grp", "seg"), None, None),
        P("grp", "seg", None),
        P("grp", "seg", None),
        P("grp", "seg", None),
        P("grp", "seg", None),
    )
    return jax.shard_map(step, mesh=mesh, in_specs=in_specs, out_specs=out_specs, check_vma=False)
```

```python
import functools

import jax
import jax.numpy as jnp
from jax import lax
from jax.experimental import pallas as pl
from jax.experimental.pallas import tpu as pltpu
from jax.sharding import PartitionSpec as P


PIECES = 4
TOP = 16


def gelu_parts(pre):
    act = 0.5 * pre * (1.0 + lax.erf(pre * 0.7071067811865476))
    slope = (
        0.5 * (1.0 + lax.erf(pre * 0.7071067811865476))
        + pre * jnp.exp(-0.5 * pre * pre) * 0.3989422804014327
    )
    return (act, slope)


def mix_of(route_ref):
    experts = route_ref.shape[2]
    return (route_ref[:, 0, :].astype(jnp.float32) / (8.0 * experts)).astype(jnp.bfloat16)


def spread(mix, rows, out_ref):
    lines, columns = mix.shape[0], mix.shape[1] * rows
    pick = lax.broadcasted_iota(jnp.int32, (mix.shape[1], columns), 1) // rows
    pick = pick == lax.broadcasted_iota(jnp.int32, (mix.shape[1], columns), 0)
    pick = jnp.where(pick, 1.0, 0.0).astype(jnp.bfloat16)
    wide = jnp.dot(mix, pick, preferred_element_type=jnp.float32)
    same = lax.broadcasted_iota(jnp.int32, (rows, columns), 0)
    same = same == lax.broadcasted_iota(jnp.int32, (rows, columns), 1) % rows
    for i in range(lines):
        line = jnp.broadcast_to(wide[i : i + 1, :], (rows, columns))
        out_ref[i * rows : (i + 1) * rows, :] = jnp.where(same, line, 0.0).astype(jnp.bfloat16)


def mix_kernel(rows, top, resident, me_ref, route_ref, weight_ref, *refs):
    outs, (mixer_ref, sum_ref, held_ref, in_sem, sems) = refs[:-5], refs[-5:]
    if not resident:
        fetched = pltpu.make_async_copy(weight_ref, held_ref, in_sem)
        fetched.start()
    mix = mix_of(route_ref)
    segs = mix.shape[0]
    if top:
        line = lax.broadcasted_iota(jnp.int32, (segs, segs), 0)
        apart = (line % top) * (segs // top) + line // top
        chosen = lax.broadcasted_iota(jnp.int32, (segs, segs), 1) == (apart ^ me_ref[0])
        chosen = jnp.where(chosen, 1.0, 0.0).astype(jnp.bfloat16)
        mix = jnp.dot(chosen, mix, preferred_element_type=jnp.float32).astype(jnp.bfloat16)
    spread(mix, rows, mixer_ref)
    if not resident:
        fetched.wait()
        weight_ref = held_ref
    size = sum_ref.shape[0] // sems.shape[0]
    lines = outs[0].shape[0]
    copies = []
    for i in range(sems.shape[0]):
        here = slice(i * size, (i + 1) * size)
        sums = jnp.dot(mixer_ref[here, :], weight_ref[...], preferred_element_type=jnp.float32)
        sum_ref[here, :] = sums.astype(jnp.bfloat16)
        place = pl.ds(i * size % lines, size)
        copy = pltpu.make_async_copy(
            sum_ref.at[here, :], outs[i * size // lines].at[place, :], sems.at[i]
        )
        copy.start()
        copies.append(copy)
    for copy in copies:
        copy.wait()


def mix_call(me, routes, weights, parts, top, resident):
    segs = routes.shape[0]
    experts, rows, width = weights.shape
    lines = segs * rows // parts
    steps = max(4, parts)
    weights = weights.reshape(experts * rows, width)
    whole, free = pl.BlockSpec(memory_space=pltpu.VMEM), pl.BlockSpec(memory_space=pl.ANY)
    if not resident:
        weights = pltpu.with_memory_space_constraint(weights, pltpu.HBM)
    return pl.pallas_call(
        functools.partial(mix_kernel, rows, top, resident),
        in_specs=[pl.BlockSpec(memory_space=pltpu.SMEM), whole, whole if resident else free],
        out_specs=[free] * parts,
        out_shape=[
            (pltpu.VMEM if top and i == 0 else pltpu.HBM)((lines, width), jnp.bfloat16)
            for i in range(parts)
        ],
        scratch_shapes=[
            pltpu.VMEM((segs * rows, experts * rows), jnp.bfloat16),
            pltpu.VMEM((segs * rows, width), jnp.bfloat16),
            pltpu.VMEM((8, 128) if resident else (experts * rows, width), jnp.bfloat16),
            pltpu.SemaphoreType.DMA,
            pltpu.SemaphoreType.DMA((steps,)),
        ],
        compiler_params=pltpu.CompilerParams(vmem_limit_bytes=10 << 20),
        name="mix",
    )(me, routes, weights)


def turn_kernel(rows, route_ref, out_ref):
    spread(mix_of(route_ref).astype(jnp.float32).T.astype(jnp.bfloat16), rows, out_ref)


def turn(routes, rows):
    segs, _, experts = routes.shape
    return pl.pallas_call(
        functools.partial(turn_kernel, rows),
        out_shape=jax.ShapeDtypeStruct((experts * rows, segs * rows), jnp.bfloat16),
        compiler_params=pltpu.CompilerParams(vmem_limit_bytes=8 << 20),
        name="turn",
    )(routes)


def copy_all(copies):
    for copy in copies:
        copy.start()
    for copy in copies:
        copy.wait()


def regroup_kernel(low, top, rows, *refs):
    plane, send = refs[:low], refs[low:]
    for z in range(1, top):
        for k in range(low):
            send[z - 1][k * rows : (k + 1) * rows, :] = plane[k][z * rows : (z + 1) * rows, :]


def settle_kernel(low, top, rows, me_ref, *refs):
    plane, got, out_ref, sems = refs[:low], refs[low : low + top - 1], refs[-2], refs[-1]
    copies = []
    for z in range(top):
        for k in range(low):
            source = plane[k].at[pl.ds(0, rows), :]
            if z:
                source = got[z - 1].at[pl.ds(k * rows, rows), :]
            place = pl.multiple_of((me_ref[0] ^ (z * low + k)) * rows, rows)
            copies.append(
                pltpu.make_async_copy(source, out_ref.at[pl.ds(place, rows), :], sems.at[k, z])
            )
    copy_all(copies)


def by_permutes(me, parts, segs, rows, top):
    low = segs // top
    width = parts[0].shape[1]
    hbm, free = pl.BlockSpec(memory_space=pltpu.HBM), pl.BlockSpec(memory_space=pl.ANY)
    near = pl.BlockSpec(memory_space=pltpu.VMEM)

    def swap(block, apart):
        return lax.ppermute(block, "seg", [(i, i ^ apart) for i in range(segs)])

    plane = [parts[0]] + [swap(parts[k], k) for k in range(1, low)]
    send = pl.pallas_call(
        functools.partial(regroup_kernel, low, top, rows),
        in_specs=[near] * low,
        out_specs=[near] * (top - 1),
        out_shape=[pltpu.VMEM((low * rows, width), jnp.bfloat16)] * (top - 1),
        compiler_params=pltpu.CompilerParams(vmem_limit_bytes=4 << 20),
        name="regroup",
    )(*plane)
    got = [swap(send[z - 1], z * low) for z in reversed(range(1, top))][::-1]
    return pl.pallas_call(
        functools.partial(settle_kernel, low, top, rows),
        in_specs=[pl.BlockSpec(memory_space=pltpu.SMEM)] + [free] * (low + top - 1),
        out_specs=hbm,
        out_shape=pltpu.HBM((segs * rows, width), jnp.bfloat16),
        scratch_shapes=[pltpu.SemaphoreType.DMA((low, top))],
        compiler_params=pltpu.CompilerParams(vmem_limit_bytes=1 << 20),
        name="settle",
    )(me, *plane, *got)


def fetch_kernel(count, *refs):
    sources, targets, sems = refs[:count], refs[count : 2 * count], refs[2 * count]
    copies = [
        pltpu.make_async_copy(source, target, sems.at[i])
        for i, (source, target) in enumerate(zip(sources, targets))
    ]
    for copy in copies:
        copy.start()
    for copy in copies:
        copy.wait()


def fetch(*arrays):
    count = len(arrays)
    return pl.pallas_call(
        functools.partial(fetch_kernel, count),
        in_specs=[pl.BlockSpec(memory_space=pltpu.HBM)] * count,
        out_specs=[pl.BlockSpec(memory_space=pltpu.VMEM)] * count,
        out_shape=[pltpu.VMEM(array.shape, array.dtype) for array in arrays],
        scratch_shapes=[pltpu.SemaphoreType.DMA((count,))],
        compiler_params=pltpu.CompilerParams(vmem_limit_bytes=1 << 20),
        name="fetch",
    )(*(pltpu.with_memory_space_constraint(array, pltpu.HBM) for array in arrays))


def update_kernel(
    count, rows, route_ref, grad_ref, weight_ref, momentum_hbm, new_momentum_hbm, new_hbm,
    mixer_ref, momentum_ref, new_ref, in_sems, out_sems,
):
    lines = momentum_ref.shape[0] // count
    parts = [slice(i * lines, (i + 1) * lines) for i in range(count)]
    reads = [
        pltpu.make_async_copy(momentum_hbm.at[here, :], momentum_ref.at[here, :], in_sems.at[i])
        for i, here in enumerate(parts)
    ]
    for read in reads:
        read.start()
    turn_kernel(rows, route_ref, mixer_ref)
    writes = []
    for i, here in enumerate(parts):
        part = jnp.dot(mixer_ref[here, :], grad_ref[...], preferred_element_type=jnp.float32)
        reads[i].wait()
        moved = 0.9 * momentum_ref[here, :] + part
        momentum_ref[here, :] = moved
        rounded = weight_ref[here, :].astype(jnp.float32) - 0.01 * moved
        new_ref[here, :] = rounded.astype(jnp.bfloat16)
        pairs = ((momentum_ref, new_momentum_hbm), (new_ref, new_hbm))
        for j, (source, target) in enumerate(pairs):
            write = pltpu.make_async_copy(source.at[here, :], target.at[here, :], out_sems.at[i, j])
            write.start()
            writes.append(write)
    for write in writes:
        write.wait()


def update_last(routes, grads, weights, momentum):
    experts, rows, width = weights.shape
    lines = experts * rows
    count = PIECES if experts % PIECES == 0 else 1
    weights = pltpu.with_memory_space_constraint(weights.reshape(lines, width), pltpu.VMEM)
    grads = pltpu.with_memory_space_constraint(grads, pltpu.VMEM)
    momentum = pltpu.with_memory_space_constraint(momentum.reshape(lines, width), pltpu.HBM)
    vmem, hbm = pl.BlockSpec(memory_space=pltpu.VMEM), pl.BlockSpec(memory_space=pltpu.HBM)
    new_momentum, new = pl.pallas_call(
        functools.partial(update_kernel, count, rows),
        in_specs=[vmem, vmem, vmem, hbm],
        out_specs=[hbm, hbm],
        out_shape=[
            jax.ShapeDtypeStruct((lines, width), jnp.float32),
            jax.ShapeDtypeStruct((lines, width), jnp.bfloat16),
        ],
        scratch_shapes=[
            pltpu.VMEM((lines, grads.shape[0]), jnp.bfloat16),
            pltpu.VMEM((lines, width), jnp.float32),
            pltpu.VMEM((lines, width), jnp.bfloat16),
            pltpu.SemaphoreType.DMA((count,)),
            pltpu.SemaphoreType.DMA((count, 2)),
        ],
        compiler_params=pltpu.CompilerParams(vmem_limit_bytes=14 << 20),
        name="update_last",
    )(routes, grads, weights, momentum)
    return new_momentum.reshape(experts, rows, width), new.reshape(experts, rows, width)


def exchange(blocks):
    return lax.all_to_all(blocks, "seg", split_axis=0, concat_axis=0, tiled=True)


def step(tokens, cotangent, routing, w_up, w_down, momentum_up, momentum_down):
    group_count = lax.axis_size("grp")
    seg_count = lax.axis_size("seg")
    group_index = lax.axis_index("grp")
    experts, slice_rows, width = w_up.shape
    owned = experts // group_count
    hidden = seg_count * slice_rows

    routes = exchange(jnp.broadcast_to(routing[:, None, :], (seg_count, 1, experts)))
    me = lax.axis_index("seg").astype(jnp.int32)[None]
    (early_up,) = fetch(w_up)
    first = mix_call(me, routes, early_up, 1, 0, True)[0]

    def delivered(sums):
        return exchange(sums.reshape(seg_count, slice_rows, width)).reshape(hidden, width)

    def returned(grads):
        return delivered(grads.astype(jnp.bfloat16))

    turned = turn(routes, slice_rows)

    def updated(weights, momentum, grads):
        part = jnp.dot(turned, grads, preferred_element_type=jnp.float32)
        part = part.reshape(experts, slice_rows, width)
        if group_count > 1:
            part = part.astype(jnp.bfloat16)
            part = lax.psum_scatter(part, "grp", scatter_dimension=0, tiled=True)
            part = part.astype(jnp.float32)
            weights = lax.dynamic_slice_in_dim(weights, group_index * owned, owned, 0)
        new_momentum = 0.9 * momentum + part
        new = (weights.astype(jnp.float32) - 0.01 * new_momentum).astype(jnp.bfloat16)
        return new_momentum, new

    inputs = tokens[0]
    grads = cotangent[0]
    up = delivered(first)
    top = TOP if seg_count % TOP == 0 and seg_count & (seg_count - 1) == 0 else 0
    if top:
        parts = mix_call(me, routes, w_down, seg_count // top, top, False)
        down = by_permutes(me, parts, seg_count, slice_rows, top)
    else:
        down = delivered(mix_call(me, routes, w_down, 1, 0, False)[0])
    pre = lax.dot_general(inputs, up, (((1,), (1,)), ((), ())), preferred_element_type=jnp.float32)
    act_full, slope = gelu_parts(pre)
    act = act_full.astype(jnp.bfloat16)
    grad_down = returned(
        lax.dot_general(act, grads, (((0,), (0,)), ((), ())), preferred_element_type=jnp.float32),
    )
    d_act = lax.dot_general(
        grads, down, (((1,), (1,)), ((), ())), preferred_element_type=jnp.float32
    )
    d_pre = (d_act * slope).astype(jnp.bfloat16)
    grad_up = returned(
        lax.dot_general(d_pre, inputs, (((0,), (0,)), ((), ())), preferred_element_type=jnp.float32),
    )
    new_momentum_down, new_down = updated(w_down, momentum_down, grad_down)
    act, d_pre, new_momentum_down, new_down = lax.optimization_barrier(
        (act, d_pre, new_momentum_down, new_down)
    )
    layer_out = jnp.dot(act, down, preferred_element_type=jnp.float32).astype(jnp.bfloat16)
    token_grad = jnp.dot(d_pre, up, preferred_element_type=jnp.float32).astype(jnp.bfloat16)
    layer_out, token_grad, late_up = lax.optimization_barrier((layer_out, token_grad, w_up))
    if group_count == 1:
        (late_up,) = fetch(late_up)
        new_momentum_up, new_up = update_last(routes, grad_up, late_up, momentum_up)
    else:
        new_momentum_up, new_up = updated(late_up, momentum_up, grad_up)
    return (layer_out[None], token_grad[None], new_momentum_up, new_momentum_down, new_up, new_down)


def solution(mesh):
    in_specs = (
        P(("grp", "seg"), None, None),
        P(("grp", "seg"), None, None),
        P(("grp", "seg"), None),
        P(None, "seg", None),
        P(None, "seg", None),
        P("grp", "seg", None),
        P("grp", "seg", None),
    )
    out_specs = (
        P(("grp", "seg"), None, None),
        P(("grp", "seg"), None, None),
        P("grp", "seg", None),
        P("grp", "seg", None),
        P("grp", "seg", None),
        P("grp", "seg", None),
    )
    return jax.shard_map(step, mesh=mesh, in_specs=in_specs, out_specs=out_specs, check_vma=False)
```

```python
import functools

import jax
import jax.numpy as jnp
from jax import lax
from jax.experimental import pallas as pl
from jax.experimental.pallas import tpu as pltpu
from jax.sharding import PartitionSpec as P


PIECES = 8
STRIDE = 4
TOP = 16


def gelu_parts(pre):
    act = 0.5 * pre * (1.0 + lax.erf(pre * 0.7071067811865476))
    slope = (
        0.5 * (1.0 + lax.erf(pre * 0.7071067811865476))
        + pre * jnp.exp(-0.5 * pre * pre) * 0.3989422804014327
    )
    return (act, slope)


def mix_of(route_ref):
    experts = route_ref.shape[2]
    return (route_ref[:, 0, :].astype(jnp.float32) / (8.0 * experts)).astype(jnp.bfloat16)


def spread(mix, rows, out_ref):
    lines, columns = mix.shape[0], mix.shape[1] * rows
    pick = lax.broadcasted_iota(jnp.int32, (mix.shape[1], columns), 1) // rows
    pick = pick == lax.broadcasted_iota(jnp.int32, (mix.shape[1], columns), 0)
    pick = jnp.where(pick, 1.0, 0.0).astype(jnp.bfloat16)
    wide = jnp.dot(mix, pick, preferred_element_type=jnp.float32)
    same = lax.broadcasted_iota(jnp.int32, (rows, columns), 0)
    same = same == lax.broadcasted_iota(jnp.int32, (rows, columns), 1) % rows
    for i in range(lines):
        line = jnp.broadcast_to(wide[i : i + 1, :], (rows, columns))
        out_ref[i * rows : (i + 1) * rows, :] = jnp.where(same, line, 0.0).astype(jnp.bfloat16)


def mix_kernel(rows, top, resident, me_ref, route_ref, weight_ref, *refs):
    outs, (mixer_ref, sum_ref, held_ref, in_sem, sems) = refs[:-5], refs[-5:]
    if not resident:
        fetched = pltpu.make_async_copy(weight_ref, held_ref, in_sem)
        fetched.start()
    mix = mix_of(route_ref)
    segs = mix.shape[0]
    if top:
        line = lax.broadcasted_iota(jnp.int32, (segs, segs), 0)
        apart = (line % top) * (segs // top) + line // top
        chosen = lax.broadcasted_iota(jnp.int32, (segs, segs), 1) == (apart ^ me_ref[0])
        chosen = jnp.where(chosen, 1.0, 0.0).astype(jnp.bfloat16)
        mix = jnp.dot(chosen, mix, preferred_element_type=jnp.float32).astype(jnp.bfloat16)
    spread(mix, rows, mixer_ref)
    if not resident:
        fetched.wait()
        weight_ref = held_ref
    size = sum_ref.shape[0] // sems.shape[0]
    lines = outs[0].shape[0]
    copies = []
    for i in range(sems.shape[0]):
        here = slice(i * size, (i + 1) * size)
        sums = jnp.dot(mixer_ref[here, :], weight_ref[...], preferred_element_type=jnp.float32)
        sum_ref[here, :] = sums.astype(jnp.bfloat16)
        place = pl.ds(i * size % lines, size)
        copy = pltpu.make_async_copy(
            sum_ref.at[here, :], outs[i * size // lines].at[place, :], sems.at[i]
        )
        copy.start()
        copies.append(copy)
    for copy in copies:
        copy.wait()


def mix_call(me, routes, weights, parts, top, resident):
    segs = routes.shape[0]
    experts, rows, width = weights.shape
    lines = segs * rows // parts
    steps = max(4, parts)
    weights = weights.reshape(experts * rows, width)
    whole, free = pl.BlockSpec(memory_space=pltpu.VMEM), pl.BlockSpec(memory_space=pl.ANY)
    if not resident:
        weights = pltpu.with_memory_space_constraint(weights, pltpu.HBM)
    return pl.pallas_call(
        functools.partial(mix_kernel, rows, top, resident),
        in_specs=[pl.BlockSpec(memory_space=pltpu.SMEM), whole, whole if resident else free],
        out_specs=[free] * parts,
        out_shape=[
            (pltpu.VMEM if top and i == 0 else pltpu.HBM)((lines, width), jnp.bfloat16)
            for i in range(parts)
        ],
        scratch_shapes=[
            pltpu.VMEM((segs * rows, experts * rows), jnp.bfloat16),
            pltpu.VMEM((segs * rows, width), jnp.bfloat16),
            pltpu.VMEM((8, 128) if resident else (experts * rows, width), jnp.bfloat16),
            pltpu.SemaphoreType.DMA,
            pltpu.SemaphoreType.DMA((steps,)),
        ],
        compiler_params=pltpu.CompilerParams(vmem_limit_bytes=10 << 20),
        name="mix",
    )(me, routes, weights)


def turn_kernel(rows, route_ref, out_ref):
    spread(mix_of(route_ref).astype(jnp.float32).T.astype(jnp.bfloat16), rows, out_ref)


def turn(routes, rows):
    segs, _, experts = routes.shape
    return pl.pallas_call(
        functools.partial(turn_kernel, rows),
        out_shape=jax.ShapeDtypeStruct((experts * rows, segs * rows), jnp.bfloat16),
        compiler_params=pltpu.CompilerParams(vmem_limit_bytes=8 << 20),
        name="turn",
    )(routes)


def copy_all(copies):
    for copy in copies:
        copy.start()
    for copy in copies:
        copy.wait()


def regroup_kernel(low, top, rows, *refs):
    plane, send = refs[:low], refs[low:]
    for z in range(1, top):
        for k in range(low):
            send[z - 1][k * rows : (k + 1) * rows, :] = plane[k][z * rows : (z + 1) * rows, :]


def settle_kernel(low, top, rows, me_ref, *refs):
    plane, got, out_ref, sems = refs[:low], refs[low : low + top - 1], refs[-2], refs[-1]
    copies = []
    for z in range(top):
        for k in range(low):
            source = plane[k].at[pl.ds(0, rows), :]
            if z:
                source = got[z - 1].at[pl.ds(k * rows, rows), :]
            place = pl.multiple_of((me_ref[0] ^ (z * low + k)) * rows, rows)
            copies.append(
                pltpu.make_async_copy(source, out_ref.at[pl.ds(place, rows), :], sems.at[k, z])
            )
    copy_all(copies)


def by_permutes(me, parts, segs, rows, top):
    low = segs // top
    width = parts[0].shape[1]
    hbm, free = pl.BlockSpec(memory_space=pltpu.HBM), pl.BlockSpec(memory_space=pl.ANY)
    near = pl.BlockSpec(memory_space=pltpu.VMEM)

    def swap(block, apart):
        return lax.ppermute(block, "seg", [(i, i ^ apart) for i in range(segs)])

    plane = [parts[0]] + [swap(parts[k], k) for k in range(1, low)]
    send = pl.pallas_call(
        functools.partial(regroup_kernel, low, top, rows),
        in_specs=[near] * low,
        out_specs=[near] * (top - 1),
        out_shape=[pltpu.VMEM((low * rows, width), jnp.bfloat16)] * (top - 1),
        compiler_params=pltpu.CompilerParams(vmem_limit_bytes=4 << 20),
        name="regroup",
    )(*plane)
    got = [swap(send[z - 1], z * low) for z in reversed(range(1, top))][::-1]
    return pl.pallas_call(
        functools.partial(settle_kernel, low, top, rows),
        in_specs=[pl.BlockSpec(memory_space=pltpu.SMEM)] + [free] * (low + top - 1),
        out_specs=hbm,
        out_shape=pltpu.HBM((segs * rows, width), jnp.bfloat16),
        scratch_shapes=[pltpu.SemaphoreType.DMA((low, top))],
        compiler_params=pltpu.CompilerParams(vmem_limit_bytes=1 << 20),
        name="settle",
    )(me, *plane, *got)


def fetch_kernel(count, *refs):
    sources, targets, sems = refs[:count], refs[count : 2 * count], refs[2 * count]
    copies = [
        pltpu.make_async_copy(source, target, sems.at[i])
        for i, (source, target) in enumerate(zip(sources, targets))
    ]
    for copy in copies:
        copy.start()
    for copy in copies:
        copy.wait()


def fetch(*arrays):
    count = len(arrays)
    return pl.pallas_call(
        functools.partial(fetch_kernel, count),
        in_specs=[pl.BlockSpec(memory_space=pltpu.HBM)] * count,
        out_specs=[pl.BlockSpec(memory_space=pltpu.VMEM)] * count,
        out_shape=[pltpu.VMEM(array.shape, array.dtype) for array in arrays],
        scratch_shapes=[pltpu.SemaphoreType.DMA((count,))],
        compiler_params=pltpu.CompilerParams(vmem_limit_bytes=1 << 20),
        name="fetch",
    )(*(pltpu.with_memory_space_constraint(array, pltpu.HBM) for array in arrays))


def update_kernel(
    count, rows, route_ref, grad_ref, weight_ref, momentum_hbm, new_momentum_hbm, new_hbm,
    mixer_ref, part_ref, momentum_ref, new_ref, in_sems, out_sems,
):
    lines = momentum_ref.shape[0] // count
    parts = [slice(i * lines, (i + 1) * lines) for i in range(count)]
    reads = [
        pltpu.make_async_copy(momentum_hbm.at[here, :], momentum_ref.at[here, :], in_sems.at[i])
        for i, here in enumerate(parts)
    ]
    for read in reads:
        read.start()
    turn_kernel(rows, route_ref, mixer_ref)
    writes = []
    stride = min(STRIDE, count)
    for i, here in enumerate(parts):
        if i % stride == 0:
            ahead = slice(i * lines, (i + stride) * lines)
            part_ref[ahead, :] = jnp.dot(
                mixer_ref[ahead, :], grad_ref[...], preferred_element_type=jnp.float32
            )
        reads[i].wait()
        moved = 0.9 * momentum_ref[here, :] + part_ref[here, :]
        momentum_ref[here, :] = moved
        rounded = weight_ref[here, :].astype(jnp.float32) - 0.01 * moved
        new_ref[here, :] = rounded.astype(jnp.bfloat16)
        pairs = ((momentum_ref, new_momentum_hbm), (new_ref, new_hbm))
        for j, (source, target) in enumerate(pairs):
            write = pltpu.make_async_copy(source.at[here, :], target.at[here, :], out_sems.at[i, j])
            write.start()
            writes.append(write)
    for write in writes:
        write.wait()


def update_last(routes, grads, weights, momentum):
    experts, rows, width = weights.shape
    lines = experts * rows
    count = PIECES if experts % PIECES == 0 else 1
    weights = pltpu.with_memory_space_constraint(weights.reshape(lines, width), pltpu.VMEM)
    grads = pltpu.with_memory_space_constraint(grads, pltpu.VMEM)
    momentum = pltpu.with_memory_space_constraint(momentum.reshape(lines, width), pltpu.HBM)
    vmem, hbm = pl.BlockSpec(memory_space=pltpu.VMEM), pl.BlockSpec(memory_space=pltpu.HBM)
    new_momentum, new = pl.pallas_call(
        functools.partial(update_kernel, count, rows),
        in_specs=[vmem, vmem, vmem, hbm],
        out_specs=[hbm, hbm],
        out_shape=[
            jax.ShapeDtypeStruct((lines, width), jnp.float32),
            jax.ShapeDtypeStruct((lines, width), jnp.bfloat16),
        ],
        scratch_shapes=[
            pltpu.VMEM((lines, grads.shape[0]), jnp.bfloat16),
            pltpu.VMEM((lines, width), jnp.float32),
            pltpu.VMEM((lines, width), jnp.float32),
            pltpu.VMEM((lines, width), jnp.bfloat16),
            pltpu.SemaphoreType.DMA((count,)),
            pltpu.SemaphoreType.DMA((count, 2)),
        ],
        compiler_params=pltpu.CompilerParams(vmem_limit_bytes=20 << 20),
        name="update_last",
    )(routes, grads, weights, momentum)
    return new_momentum.reshape(experts, rows, width), new.reshape(experts, rows, width)


def exchange(blocks):
    return lax.all_to_all(blocks, "seg", split_axis=0, concat_axis=0, tiled=True)


def step(tokens, cotangent, routing, w_up, w_down, momentum_up, momentum_down):
    group_count = lax.axis_size("grp")
    seg_count = lax.axis_size("seg")
    group_index = lax.axis_index("grp")
    experts, slice_rows, width = w_up.shape
    owned = experts // group_count
    hidden = seg_count * slice_rows

    routes = exchange(jnp.broadcast_to(routing[:, None, :], (seg_count, 1, experts)))
    me = lax.axis_index("seg").astype(jnp.int32)[None]
    (early_up,) = fetch(w_up)
    first = mix_call(me, routes, early_up, 1, 0, True)[0]

    def delivered(sums):
        return exchange(sums.reshape(seg_count, slice_rows, width)).reshape(hidden, width)

    def returned(grads):
        return delivered(grads.astype(jnp.bfloat16))

    turned = turn(routes, slice_rows)

    def updated(weights, momentum, grads):
        part = jnp.dot(turned, grads, preferred_element_type=jnp.float32)
        part = part.reshape(experts, slice_rows, width)
        if group_count > 1:
            part = part.astype(jnp.bfloat16)
            part = lax.psum_scatter(part, "grp", scatter_dimension=0, tiled=True)
            part = part.astype(jnp.float32)
            weights = lax.dynamic_slice_in_dim(weights, group_index * owned, owned, 0)
        new_momentum = 0.9 * momentum + part
        new = (weights.astype(jnp.float32) - 0.01 * new_momentum).astype(jnp.bfloat16)
        return new_momentum, new

    inputs = tokens[0]
    grads = cotangent[0]
    up = delivered(first)
    top = TOP if seg_count % TOP == 0 and seg_count & (seg_count - 1) == 0 else 0
    if top:
        parts = mix_call(me, routes, w_down, seg_count // top, top, False)
        down = by_permutes(me, parts, seg_count, slice_rows, top)
    else:
        down = delivered(mix_call(me, routes, w_down, 1, 0, False)[0])
    pre = lax.dot_general(inputs, up, (((1,), (1,)), ((), ())), preferred_element_type=jnp.float32)
    act_full, slope = gelu_parts(pre)
    act = act_full.astype(jnp.bfloat16)
    grad_down = returned(
        lax.dot_general(act, grads, (((0,), (0,)), ((), ())), preferred_element_type=jnp.float32),
    )
    d_act = lax.dot_general(
        grads, down, (((1,), (1,)), ((), ())), preferred_element_type=jnp.float32
    )
    d_pre = (d_act * slope).astype(jnp.bfloat16)
    grad_up = returned(
        lax.dot_general(d_pre, inputs, (((0,), (0,)), ((), ())), preferred_element_type=jnp.float32),
    )
    new_momentum_down, new_down = updated(w_down, momentum_down, grad_down)
    act, d_pre, new_momentum_down, new_down = lax.optimization_barrier(
        (act, d_pre, new_momentum_down, new_down)
    )
    layer_out = jnp.dot(act, down, preferred_element_type=jnp.float32).astype(jnp.bfloat16)
    token_grad = jnp.dot(d_pre, up, preferred_element_type=jnp.float32).astype(jnp.bfloat16)
    layer_out, token_grad, late_up = lax.optimization_barrier((layer_out, token_grad, w_up))
    if group_count == 1:
        (late_up,) = fetch(late_up)
        new_momentum_up, new_up = update_last(routes, grad_up, late_up, momentum_up)
    else:
        new_momentum_up, new_up = updated(late_up, momentum_up, grad_up)
    return (layer_out[None], token_grad[None], new_momentum_up, new_momentum_down, new_up, new_down)


def solution(mesh):
    in_specs = (
        P(("grp", "seg"), None, None),
        P(("grp", "seg"), None, None),
        P(("grp", "seg"), None),
        P(None, "seg", None),
        P(None, "seg", None),
        P("grp", "seg", None),
        P("grp", "seg", None),
    )
    out_specs = (
        P(("grp", "seg"), None, None),
        P(("grp", "seg"), None, None),
        P("grp", "seg", None),
        P("grp", "seg", None),
        P("grp", "seg", None),
        P("grp", "seg", None),
    )
    return jax.shard_map(step, mesh=mesh, in_specs=in_specs, out_specs=out_specs, check_vma=False)
```

```python
import functools

import jax
import jax.numpy as jnp
from jax import lax
from jax.experimental import pallas as pl
from jax.experimental.pallas import tpu as pltpu
from jax.sharding import PartitionSpec as P


PIECES = 8
STRIDE = 4
TOP = 16


def gelu(pre):
    return 0.5 * pre * (1.0 + lax.erf(pre * 0.7071067811865476))


def gelu_slope(pre):
    return (
        0.5 * (1.0 + lax.erf(pre * 0.7071067811865476))
        + pre * jnp.exp(-0.5 * pre * pre) * 0.3989422804014327
    )


def mix_of(route_ref):
    experts = route_ref.shape[2]
    return (route_ref[:, 0, :].astype(jnp.float32) / (8.0 * experts)).astype(jnp.bfloat16)


def spread(mix, rows, out_ref):
    lines, columns = mix.shape[0], mix.shape[1] * rows
    pick = lax.broadcasted_iota(jnp.int32, (mix.shape[1], columns), 1) // rows
    pick = pick == lax.broadcasted_iota(jnp.int32, (mix.shape[1], columns), 0)
    pick = jnp.where(pick, 1.0, 0.0).astype(jnp.bfloat16)
    wide = jnp.dot(mix, pick, preferred_element_type=jnp.float32)
    same = lax.broadcasted_iota(jnp.int32, (rows, columns), 0)
    same = same == lax.broadcasted_iota(jnp.int32, (rows, columns), 1) % rows
    for i in range(lines):
        line = jnp.broadcast_to(wide[i : i + 1, :], (rows, columns))
        out_ref[i * rows : (i + 1) * rows, :] = jnp.where(same, line, 0.0).astype(jnp.bfloat16)


def mix_kernel(rows, top, resident, me_ref, route_ref, weight_ref, *refs):
    outs, (mixer_ref, sum_ref, held_ref, in_sem, sems) = refs[:-5], refs[-5:]
    if not resident:
        fetched = pltpu.make_async_copy(weight_ref, held_ref, in_sem)
        fetched.start()
    mix = mix_of(route_ref)
    segs = mix.shape[0]
    if top:
        line = lax.broadcasted_iota(jnp.int32, (segs, segs), 0)
        apart = (line % top) * (segs // top) + line // top
        chosen = lax.broadcasted_iota(jnp.int32, (segs, segs), 1) == (apart ^ me_ref[0])
        chosen = jnp.where(chosen, 1.0, 0.0).astype(jnp.bfloat16)
        mix = jnp.dot(chosen, mix, preferred_element_type=jnp.float32).astype(jnp.bfloat16)
    spread(mix, rows, mixer_ref)
    if not resident:
        fetched.wait()
        weight_ref = held_ref
    size = sum_ref.shape[0] // sems.shape[0]
    lines = outs[0].shape[0]
    copies = []
    for i in range(sems.shape[0]):
        here = slice(i * size, (i + 1) * size)
        sums = jnp.dot(mixer_ref[here, :], weight_ref[...], preferred_element_type=jnp.float32)
        sum_ref[here, :] = sums.astype(jnp.bfloat16)
        place = pl.ds(i * size % lines, size)
        copy = pltpu.make_async_copy(
            sum_ref.at[here, :], outs[i * size // lines].at[place, :], sems.at[i]
        )
        copy.start()
        copies.append(copy)
    for copy in copies:
        copy.wait()


def mix_call(me, routes, weights, parts, top, resident):
    segs = routes.shape[0]
    experts, rows, width = weights.shape
    lines = segs * rows // parts
    steps = max(4, parts)
    weights = weights.reshape(experts * rows, width)
    whole, free = pl.BlockSpec(memory_space=pltpu.VMEM), pl.BlockSpec(memory_space=pl.ANY)
    if not resident:
        weights = pltpu.with_memory_space_constraint(weights, pltpu.HBM)
    return pl.pallas_call(
        functools.partial(mix_kernel, rows, top, resident),
        in_specs=[pl.BlockSpec(memory_space=pltpu.SMEM), whole, whole if resident else free],
        out_specs=[free] * parts,
        out_shape=[
            (pltpu.VMEM if top and i == 0 else pltpu.HBM)((lines, width), jnp.bfloat16)
            for i in range(parts)
        ],
        scratch_shapes=[
            pltpu.VMEM((segs * rows, experts * rows), jnp.bfloat16),
            pltpu.VMEM((segs * rows, width), jnp.bfloat16),
            pltpu.VMEM((8, 128) if resident else (experts * rows, width), jnp.bfloat16),
            pltpu.SemaphoreType.DMA,
            pltpu.SemaphoreType.DMA((steps,)),
        ],
        compiler_params=pltpu.CompilerParams(vmem_limit_bytes=10 << 20),
        name="mix",
    )(me, routes, weights)


def turn_kernel(rows, route_ref, out_ref):
    spread(mix_of(route_ref).astype(jnp.float32).T.astype(jnp.bfloat16), rows, out_ref)


def turn(routes, rows):
    segs, _, experts = routes.shape
    return pl.pallas_call(
        functools.partial(turn_kernel, rows),
        out_shape=jax.ShapeDtypeStruct((experts * rows, segs * rows), jnp.bfloat16),
        compiler_params=pltpu.CompilerParams(vmem_limit_bytes=8 << 20),
        name="turn",
    )(routes)


def copy_all(copies):
    for copy in copies:
        copy.start()
    for copy in copies:
        copy.wait()


def regroup_kernel(low, top, rows, *refs):
    plane, send = refs[:low], refs[low:]
    for z in range(1, top):
        for k in range(low):
            send[z - 1][k * rows : (k + 1) * rows, :] = plane[k][z * rows : (z + 1) * rows, :]


def settle_kernel(low, top, rows, me_ref, *refs):
    plane, got, out_ref, sems = refs[:low], refs[low : low + top - 1], refs[-2], refs[-1]
    copies = []
    for z in range(top):
        for k in range(low):
            source = plane[k].at[pl.ds(0, rows), :]
            if z:
                source = got[z - 1].at[pl.ds(k * rows, rows), :]
            place = pl.multiple_of((me_ref[0] ^ (z * low + k)) * rows, rows)
            copies.append(
                pltpu.make_async_copy(source, out_ref.at[pl.ds(place, rows), :], sems.at[k, z])
            )
    copy_all(copies)


def by_permutes(me, parts, segs, rows, top):
    low = segs // top
    width = parts[0].shape[1]
    hbm, free = pl.BlockSpec(memory_space=pltpu.HBM), pl.BlockSpec(memory_space=pl.ANY)
    near = pl.BlockSpec(memory_space=pltpu.VMEM)

    def swap(block, apart):
        return lax.ppermute(block, "seg", [(i, i ^ apart) for i in range(segs)])

    plane = [parts[0]] + [swap(parts[k], k) for k in range(1, low)]
    send = pl.pallas_call(
        functools.partial(regroup_kernel, low, top, rows),
        in_specs=[near] * low,
        out_specs=[near] * (top - 1),
        out_shape=[pltpu.VMEM((low * rows, width), jnp.bfloat16)] * (top - 1),
        compiler_params=pltpu.CompilerParams(vmem_limit_bytes=4 << 20),
        name="regroup",
    )(*plane)
    got = [swap(send[z - 1], z * low) for z in reversed(range(1, top))][::-1]
    return pl.pallas_call(
        functools.partial(settle_kernel, low, top, rows),
        in_specs=[pl.BlockSpec(memory_space=pltpu.SMEM)] + [free] * (low + top - 1),
        out_specs=hbm,
        out_shape=pltpu.HBM((segs * rows, width), jnp.bfloat16),
        scratch_shapes=[pltpu.SemaphoreType.DMA((low, top))],
        compiler_params=pltpu.CompilerParams(vmem_limit_bytes=1 << 20),
        name="settle",
    )(me, *plane, *got)


def fetch_kernel(count, *refs):
    sources, targets, sems = refs[:count], refs[count : 2 * count], refs[2 * count]
    copies = [
        pltpu.make_async_copy(source, target, sems.at[i])
        for i, (source, target) in enumerate(zip(sources, targets))
    ]
    for copy in copies:
        copy.start()
    for copy in copies:
        copy.wait()


def fetch(*arrays):
    count = len(arrays)
    return pl.pallas_call(
        functools.partial(fetch_kernel, count),
        in_specs=[pl.BlockSpec(memory_space=pltpu.HBM)] * count,
        out_specs=[pl.BlockSpec(memory_space=pltpu.VMEM)] * count,
        out_shape=[pltpu.VMEM(array.shape, array.dtype) for array in arrays],
        scratch_shapes=[pltpu.SemaphoreType.DMA((count,))],
        compiler_params=pltpu.CompilerParams(vmem_limit_bytes=1 << 20),
        name="fetch",
    )(*(pltpu.with_memory_space_constraint(array, pltpu.HBM) for array in arrays))


def update_kernel(
    count, rows, route_ref, grad_ref, weight_ref, momentum_hbm, new_momentum_hbm, new_hbm,
    mixer_ref, part_ref, momentum_ref, new_ref, in_sems, out_sems,
):
    lines = momentum_ref.shape[0] // count
    parts = [slice(i * lines, (i + 1) * lines) for i in range(count)]
    reads = [
        pltpu.make_async_copy(momentum_hbm.at[here, :], momentum_ref.at[here, :], in_sems.at[i])
        for i, here in enumerate(parts)
    ]
    for read in reads:
        read.start()
    turn_kernel(rows, route_ref, mixer_ref)
    writes = []
    stride = min(STRIDE, count)
    for i, here in enumerate(parts):
        if i % stride == 0:
            ahead = slice(i * lines, (i + stride) * lines)
            part_ref[ahead, :] = jnp.dot(
                mixer_ref[ahead, :], grad_ref[...], preferred_element_type=jnp.float32
            )
        reads[i].wait()
        moved = 0.9 * momentum_ref[here, :] + part_ref[here, :]
        momentum_ref[here, :] = moved
        rounded = weight_ref[here, :].astype(jnp.float32) - 0.01 * moved
        new_ref[here, :] = rounded.astype(jnp.bfloat16)
        pairs = ((momentum_ref, new_momentum_hbm), (new_ref, new_hbm))
        for j, (source, target) in enumerate(pairs):
            write = pltpu.make_async_copy(source.at[here, :], target.at[here, :], out_sems.at[i, j])
            write.start()
            writes.append(write)
    for write in writes:
        write.wait()


def update_last(routes, grads, weights, momentum):
    experts, rows, width = weights.shape
    lines = experts * rows
    count = PIECES if experts % PIECES == 0 else 1
    weights = pltpu.with_memory_space_constraint(weights.reshape(lines, width), pltpu.VMEM)
    grads = pltpu.with_memory_space_constraint(grads, pltpu.VMEM)
    momentum = pltpu.with_memory_space_constraint(momentum.reshape(lines, width), pltpu.HBM)
    vmem, hbm = pl.BlockSpec(memory_space=pltpu.VMEM), pl.BlockSpec(memory_space=pltpu.HBM)
    new_momentum, new = pl.pallas_call(
        functools.partial(update_kernel, count, rows),
        in_specs=[vmem, vmem, vmem, hbm],
        out_specs=[hbm, hbm],
        out_shape=[
            jax.ShapeDtypeStruct((lines, width), jnp.float32),
            jax.ShapeDtypeStruct((lines, width), jnp.bfloat16),
        ],
        scratch_shapes=[
            pltpu.VMEM((lines, grads.shape[0]), jnp.bfloat16),
            pltpu.VMEM((lines, width), jnp.float32),
            pltpu.VMEM((lines, width), jnp.float32),
            pltpu.VMEM((lines, width), jnp.bfloat16),
            pltpu.SemaphoreType.DMA((count,)),
            pltpu.SemaphoreType.DMA((count, 2)),
        ],
        compiler_params=pltpu.CompilerParams(vmem_limit_bytes=20 << 20),
        name="update_last",
    )(routes, grads, weights, momentum)
    return new_momentum.reshape(experts, rows, width), new.reshape(experts, rows, width)


def exchange(blocks):
    return lax.all_to_all(blocks, "seg", split_axis=0, concat_axis=0, tiled=True)


def step(tokens, cotangent, routing, w_up, w_down, momentum_up, momentum_down):
    group_count = lax.axis_size("grp")
    seg_count = lax.axis_size("seg")
    group_index = lax.axis_index("grp")
    experts, slice_rows, width = w_up.shape
    owned = experts // group_count
    hidden = seg_count * slice_rows

    routes = exchange(jnp.broadcast_to(routing[:, None, :], (seg_count, 1, experts)))
    me = lax.axis_index("seg").astype(jnp.int32)[None]
    (early_up,) = fetch(w_up)
    first = mix_call(me, routes, early_up, 1, 0, True)[0]

    def delivered(sums):
        return exchange(sums.reshape(seg_count, slice_rows, width)).reshape(hidden, width)

    def returned(grads):
        return delivered(grads.astype(jnp.bfloat16))

    turned = turn(routes, slice_rows)

    def updated(weights, momentum, grads):
        part = jnp.dot(turned, grads, preferred_element_type=jnp.float32)
        part = part.reshape(experts, slice_rows, width)
        if group_count > 1:
            part = part.astype(jnp.bfloat16)
            part = lax.psum_scatter(part, "grp", scatter_dimension=0, tiled=True)
            part = part.astype(jnp.float32)
            weights = lax.dynamic_slice_in_dim(weights, group_index * owned, owned, 0)
        new_momentum = 0.9 * momentum + part
        new = (weights.astype(jnp.float32) - 0.01 * new_momentum).astype(jnp.bfloat16)
        return new_momentum, new

    inputs = tokens[0]
    grads = cotangent[0]
    up = delivered(first)
    top = TOP if seg_count % TOP == 0 and seg_count & (seg_count - 1) == 0 else 0
    if top:
        parts = mix_call(me, routes, w_down, seg_count // top, top, False)
        down = by_permutes(me, parts, seg_count, slice_rows, top)
    else:
        down = delivered(mix_call(me, routes, w_down, 1, 0, False)[0])
    pre = lax.dot_general(inputs, up, (((1,), (1,)), ((), ())), preferred_element_type=jnp.float32)
    act = gelu(pre).astype(jnp.bfloat16)
    kept = pre.astype(jnp.bfloat16)
    act, kept = lax.optimization_barrier((act, kept))
    grad_down = returned(
        lax.dot_general(act, grads, (((0,), (0,)), ((), ())), preferred_element_type=jnp.float32),
    )
    d_act = lax.dot_general(
        grads, down, (((1,), (1,)), ((), ())), preferred_element_type=jnp.float32
    )
    d_pre = (d_act * gelu_slope(kept.astype(jnp.float32))).astype(jnp.bfloat16)
    grad_up = returned(
        lax.dot_general(d_pre, inputs, (((0,), (0,)), ((), ())), preferred_element_type=jnp.float32),
    )
    new_momentum_down, new_down = updated(w_down, momentum_down, grad_down)
    act, d_pre, new_momentum_down, new_down = lax.optimization_barrier(
        (act, d_pre, new_momentum_down, new_down)
    )
    layer_out = jnp.dot(act, down, preferred_element_type=jnp.float32).astype(jnp.bfloat16)
    token_grad = jnp.dot(d_pre, up, preferred_element_type=jnp.float32).astype(jnp.bfloat16)
    layer_out, token_grad, late_up = lax.optimization_barrier((layer_out, token_grad, w_up))
    if group_count == 1:
        (late_up,) = fetch(late_up)
        new_momentum_up, new_up = update_last(routes, grad_up, late_up, momentum_up)
    else:
        new_momentum_up, new_up = updated(late_up, momentum_up, grad_up)
    return (layer_out[None], token_grad[None], new_momentum_up, new_momentum_down, new_up, new_down)


def solution(mesh):
    in_specs = (
        P(("grp", "seg"), None, None),
        P(("grp", "seg"), None, None),
        P(("grp", "seg"), None),
        P(None, "seg", None),
        P(None, "seg", None),
        P("grp", "seg", None),
        P("grp", "seg", None),
    )
    out_specs = (
        P(("grp", "seg"), None, None),
        P(("grp", "seg"), None, None),
        P("grp", "seg", None),
        P("grp", "seg", None),
        P("grp", "seg", None),
        P("grp", "seg", None),
    )
    return jax.shard_map(step, mesh=mesh, in_specs=in_specs, out_specs=out_specs, check_vma=False)
```

```python
import functools

import jax
import jax.numpy as jnp
from jax import lax
from jax.experimental import pallas as pl
from jax.experimental.pallas import tpu as pltpu
from jax.sharding import PartitionSpec as P


PIECES = 8
STRIDE = 4
TOP = 16


def gelu(pre):
    return 0.5 * pre * (1.0 + lax.erf(pre * 0.7071067811865476))


def gelu_slope(pre):
    return (
        0.5 * (1.0 + lax.erf(pre * 0.7071067811865476))
        + pre * jnp.exp(-0.5 * pre * pre) * 0.3989422804014327
    )


def mix_of(route_ref):
    experts = route_ref.shape[2]
    return (route_ref[:, 0, :].astype(jnp.float32) / (8.0 * experts)).astype(jnp.bfloat16)


def spread(mix, rows, out_ref):
    lines, columns = mix.shape[0], mix.shape[1] * rows
    pick = lax.broadcasted_iota(jnp.int32, (mix.shape[1], columns), 1) // rows
    pick = pick == lax.broadcasted_iota(jnp.int32, (mix.shape[1], columns), 0)
    pick = jnp.where(pick, 1.0, 0.0).astype(jnp.bfloat16)
    wide = jnp.dot(mix, pick, preferred_element_type=jnp.float32)
    same = lax.broadcasted_iota(jnp.int32, (rows, columns), 0)
    same = same == lax.broadcasted_iota(jnp.int32, (rows, columns), 1) % rows
    for i in range(lines):
        line = jnp.broadcast_to(wide[i : i + 1, :], (rows, columns))
        out_ref[i * rows : (i + 1) * rows, :] = jnp.where(same, line, 0.0).astype(jnp.bfloat16)


def mix_kernel(rows, top, resident, me_ref, route_ref, weight_ref, *refs):
    outs, (mixer_ref, sum_ref, held_ref, in_sem, sems) = refs[:-5], refs[-5:]
    if not resident:
        fetched = pltpu.make_async_copy(weight_ref, held_ref, in_sem)
        fetched.start()
    mix = mix_of(route_ref)
    segs = mix.shape[0]
    if top:
        line = lax.broadcasted_iota(jnp.int32, (segs, segs), 0)
        apart = (line % top) * (segs // top) + line // top
        chosen = lax.broadcasted_iota(jnp.int32, (segs, segs), 1) == (apart ^ me_ref[0])
        chosen = jnp.where(chosen, 1.0, 0.0).astype(jnp.bfloat16)
        mix = jnp.dot(chosen, mix, preferred_element_type=jnp.float32).astype(jnp.bfloat16)
    spread(mix, rows, mixer_ref)
    if not resident:
        fetched.wait()
        weight_ref = held_ref
    tile = sum_ref.shape[1] // sems.shape[0]
    lines = outs[0].shape[0]
    copies = []
    for i in range(sems.shape[0]):
        here = slice(i * tile, (i + 1) * tile)
        sums = jnp.dot(mixer_ref[...], weight_ref[:, here], preferred_element_type=jnp.float32)
        sum_ref[:, here] = sums.astype(jnp.bfloat16)
        for j, out in enumerate(outs):
            source = sum_ref.at[j * lines : (j + 1) * lines, here]
            copy = pltpu.make_async_copy(source, out.at[:, here], sems.at[i, j])
            copy.start()
            copies.append(copy)
    for copy in copies:
        copy.wait()


def mix_call(me, routes, weights, parts, top, resident):
    segs = routes.shape[0]
    experts, rows, width = weights.shape
    lines = segs * rows // parts
    steps = 4
    weights = weights.reshape(experts * rows, width)
    whole, free = pl.BlockSpec(memory_space=pltpu.VMEM), pl.BlockSpec(memory_space=pl.ANY)
    if not resident:
        weights = pltpu.with_memory_space_constraint(weights, pltpu.HBM)
    return pl.pallas_call(
        functools.partial(mix_kernel, rows, top, resident),
        in_specs=[pl.BlockSpec(memory_space=pltpu.SMEM), whole, whole if resident else free],
        out_specs=[free] * parts,
        out_shape=[
            (pltpu.VMEM if top and i == 0 else pltpu.HBM)((lines, width), jnp.bfloat16)
            for i in range(parts)
        ],
        scratch_shapes=[
            pltpu.VMEM((segs * rows, experts * rows), jnp.bfloat16),
            pltpu.VMEM((segs * rows, width), jnp.bfloat16),
            pltpu.VMEM((8, 128) if resident else (experts * rows, width), jnp.bfloat16),
            pltpu.SemaphoreType.DMA,
            pltpu.SemaphoreType.DMA((steps, parts)),
        ],
        compiler_params=pltpu.CompilerParams(vmem_limit_bytes=10 << 20),
        name="mix",
    )(me, routes, weights)


def turn_kernel(rows, route_ref, out_ref):
    spread(mix_of(route_ref).astype(jnp.float32).T.astype(jnp.bfloat16), rows, out_ref)


def turn(routes, rows):
    segs, _, experts = routes.shape
    return pl.pallas_call(
        functools.partial(turn_kernel, rows),
        out_shape=jax.ShapeDtypeStruct((experts * rows, segs * rows), jnp.bfloat16),
        compiler_params=pltpu.CompilerParams(vmem_limit_bytes=8 << 20),
        name="turn",
    )(routes)


def copy_all(copies):
    for copy in copies:
        copy.start()
    for copy in copies:
        copy.wait()


def regroup_kernel(low, top, rows, *refs):
    plane, send = refs[:low], refs[low:]
    for z in range(1, top):
        for k in range(low):
            send[z - 1][k * rows : (k + 1) * rows, :] = plane[k][z * rows : (z + 1) * rows, :]


def settle_kernel(low, top, rows, me_ref, *refs):
    plane, got, out_ref, sems = refs[:low], refs[low : low + top - 1], refs[-2], refs[-1]
    copies = []
    for z in range(top):
        for k in range(low):
            source = plane[k].at[pl.ds(0, rows), :]
            if z:
                source = got[z - 1].at[pl.ds(k * rows, rows), :]
            place = pl.multiple_of((me_ref[0] ^ (z * low + k)) * rows, rows)
            copies.append(
                pltpu.make_async_copy(source, out_ref.at[pl.ds(place, rows), :], sems.at[k, z])
            )
    copy_all(copies)


def by_permutes(me, parts, segs, rows, top):
    low = segs // top
    width = parts[0].shape[1]
    hbm, free = pl.BlockSpec(memory_space=pltpu.HBM), pl.BlockSpec(memory_space=pl.ANY)
    near = pl.BlockSpec(memory_space=pltpu.VMEM)

    def swap(block, apart):
        return lax.ppermute(block, "seg", [(i, i ^ apart) for i in range(segs)])

    plane = [parts[0]] + [swap(parts[k], k) for k in range(1, low)]
    send = pl.pallas_call(
        functools.partial(regroup_kernel, low, top, rows),
        in_specs=[near] * low,
        out_specs=[near] * (top - 1),
        out_shape=[pltpu.VMEM((low * rows, width), jnp.bfloat16)] * (top - 1),
        compiler_params=pltpu.CompilerParams(vmem_limit_bytes=4 << 20),
        name="regroup",
    )(*plane)
    got = [swap(send[z - 1], z * low) for z in reversed(range(1, top))][::-1]
    return pl.pallas_call(
        functools.partial(settle_kernel, low, top, rows),
        in_specs=[pl.BlockSpec(memory_space=pltpu.SMEM)] + [free] * (low + top - 1),
        out_specs=hbm,
        out_shape=pltpu.HBM((segs * rows, width), jnp.bfloat16),
        scratch_shapes=[pltpu.SemaphoreType.DMA((low, top))],
        compiler_params=pltpu.CompilerParams(vmem_limit_bytes=1 << 20),
        name="settle",
    )(me, *plane, *got)


def fetch_kernel(count, *refs):
    sources, targets, sems = refs[:count], refs[count : 2 * count], refs[2 * count]
    copies = [
        pltpu.make_async_copy(source, target, sems.at[i])
        for i, (source, target) in enumerate(zip(sources, targets))
    ]
    for copy in copies:
        copy.start()
    for copy in copies:
        copy.wait()


def fetch(*arrays):
    count = len(arrays)
    return pl.pallas_call(
        functools.partial(fetch_kernel, count),
        in_specs=[pl.BlockSpec(memory_space=pltpu.HBM)] * count,
        out_specs=[pl.BlockSpec(memory_space=pltpu.VMEM)] * count,
        out_shape=[pltpu.VMEM(array.shape, array.dtype) for array in arrays],
        scratch_shapes=[pltpu.SemaphoreType.DMA((count,))],
        compiler_params=pltpu.CompilerParams(vmem_limit_bytes=1 << 20),
        name="fetch",
    )(*(pltpu.with_memory_space_constraint(array, pltpu.HBM) for array in arrays))


def update_kernel(
    count, rows, route_ref, grad_ref, weight_ref, momentum_hbm, new_momentum_hbm, new_hbm,
    mixer_ref, part_ref, momentum_ref, new_ref, in_sems, out_sems,
):
    lines = momentum_ref.shape[0] // count
    parts = [slice(i * lines, (i + 1) * lines) for i in range(count)]
    reads = [
        pltpu.make_async_copy(momentum_hbm.at[here, :], momentum_ref.at[here, :], in_sems.at[i])
        for i, here in enumerate(parts)
    ]
    for read in reads:
        read.start()
    turn_kernel(rows, route_ref, mixer_ref)
    writes = []
    stride = min(STRIDE, count)
    for i, here in enumerate(parts):
        if i % stride == 0:
            ahead = slice(i * lines, (i + stride) * lines)
            part_ref[ahead, :] = jnp.dot(
                mixer_ref[ahead, :], grad_ref[...], preferred_element_type=jnp.float32
            )
        reads[i].wait()
        moved = 0.9 * momentum_ref[here, :] + part_ref[here, :]
        momentum_ref[here, :] = moved
        rounded = weight_ref[here, :].astype(jnp.float32) - 0.01 * moved
        new_ref[here, :] = rounded.astype(jnp.bfloat16)
        pairs = ((momentum_ref, new_momentum_hbm), (new_ref, new_hbm))
        for j, (source, target) in enumerate(pairs):
            write = pltpu.make_async_copy(source.at[here, :], target.at[here, :], out_sems.at[i, j])
            write.start()
            writes.append(write)
    for write in writes:
        write.wait()


def update_last(routes, grads, weights, momentum):
    experts, rows, width = weights.shape
    lines = experts * rows
    count = PIECES if experts % PIECES == 0 else 1
    weights = pltpu.with_memory_space_constraint(weights.reshape(lines, width), pltpu.VMEM)
    grads = pltpu.with_memory_space_constraint(grads, pltpu.VMEM)
    momentum = pltpu.with_memory_space_constraint(momentum.reshape(lines, width), pltpu.HBM)
    vmem, hbm = pl.BlockSpec(memory_space=pltpu.VMEM), pl.BlockSpec(memory_space=pltpu.HBM)
    new_momentum, new = pl.pallas_call(
        functools.partial(update_kernel, count, rows),
        in_specs=[vmem, vmem, vmem, hbm],
        out_specs=[hbm, hbm],
        out_shape=[
            jax.ShapeDtypeStruct((lines, width), jnp.float32),
            jax.ShapeDtypeStruct((lines, width), jnp.bfloat16),
        ],
        scratch_shapes=[
            pltpu.VMEM((lines, grads.shape[0]), jnp.bfloat16),
            pltpu.VMEM((lines, width), jnp.float32),
            pltpu.VMEM((lines, width), jnp.float32),
            pltpu.VMEM((lines, width), jnp.bfloat16),
            pltpu.SemaphoreType.DMA((count,)),
            pltpu.SemaphoreType.DMA((count, 2)),
        ],
        compiler_params=pltpu.CompilerParams(vmem_limit_bytes=20 << 20),
        name="update_last",
    )(routes, grads, weights, momentum)
    return new_momentum.reshape(experts, rows, width), new.reshape(experts, rows, width)


def exchange(blocks):
    return lax.all_to_all(blocks, "seg", split_axis=0, concat_axis=0, tiled=True)


def step(tokens, cotangent, routing, w_up, w_down, momentum_up, momentum_down):
    group_count = lax.axis_size("grp")
    seg_count = lax.axis_size("seg")
    group_index = lax.axis_index("grp")
    experts, slice_rows, width = w_up.shape
    owned = experts // group_count
    hidden = seg_count * slice_rows

    routes = exchange(jnp.broadcast_to(routing[:, None, :], (seg_count, 1, experts)))
    me = lax.axis_index("seg").astype(jnp.int32)[None]
    (early_up,) = fetch(w_up)
    first = mix_call(me, routes, early_up, 1, 0, True)[0]

    def delivered(sums):
        return exchange(sums.reshape(seg_count, slice_rows, width)).reshape(hidden, width)

    def returned(grads):
        return delivered(grads.astype(jnp.bfloat16))

    turned = turn(routes, slice_rows)

    def updated(weights, momentum, grads):
        part = jnp.dot(turned, grads, preferred_element_type=jnp.float32)
        part = part.reshape(experts, slice_rows, width)
        if group_count > 1:
            part = part.astype(jnp.bfloat16)
            part = lax.psum_scatter(part, "grp", scatter_dimension=0, tiled=True)
            part = part.astype(jnp.float32)
            weights = lax.dynamic_slice_in_dim(weights, group_index * owned, owned, 0)
        new_momentum = 0.9 * momentum + part
        new = (weights.astype(jnp.float32) - 0.01 * new_momentum).astype(jnp.bfloat16)
        return new_momentum, new

    inputs = tokens[0]
    grads = cotangent[0]
    up = delivered(first)
    top = TOP if seg_count % TOP == 0 and seg_count & (seg_count - 1) == 0 else 0
    if top:
        parts = mix_call(me, routes, w_down, seg_count // top, top, False)
        down = by_permutes(me, parts, seg_count, slice_rows, top)
    else:
        down = delivered(mix_call(me, routes, w_down, 1, 0, False)[0])
    pre = lax.dot_general(inputs, up, (((1,), (1,)), ((), ())), preferred_element_type=jnp.float32)
    act = gelu(pre).astype(jnp.bfloat16)
    kept = pre.astype(jnp.bfloat16)
    act, kept = lax.optimization_barrier((act, kept))
    grad_down = returned(
        lax.dot_general(act, grads, (((0,), (0,)), ((), ())), preferred_element_type=jnp.float32),
    )
    d_act = lax.dot_general(
        grads, down, (((1,), (1,)), ((), ())), preferred_element_type=jnp.float32
    )
    d_pre = (d_act * gelu_slope(kept.astype(jnp.float32))).astype(jnp.bfloat16)
    grad_up = returned(
        lax.dot_general(d_pre, inputs, (((0,), (0,)), ((), ())), preferred_element_type=jnp.float32),
    )
    new_momentum_down, new_down = updated(w_down, momentum_down, grad_down)
    act, d_pre, new_momentum_down, new_down = lax.optimization_barrier(
        (act, d_pre, new_momentum_down, new_down)
    )
    layer_out = jnp.dot(act, down, preferred_element_type=jnp.float32).astype(jnp.bfloat16)
    token_grad = jnp.dot(d_pre, up, preferred_element_type=jnp.float32).astype(jnp.bfloat16)
    layer_out, token_grad, late_up = lax.optimization_barrier((layer_out, token_grad, w_up))
    if group_count == 1:
        (late_up,) = fetch(late_up)
        new_momentum_up, new_up = update_last(routes, grad_up, late_up, momentum_up)
    else:
        new_momentum_up, new_up = updated(late_up, momentum_up, grad_up)
    return (layer_out[None], token_grad[None], new_momentum_up, new_momentum_down, new_up, new_down)


def solution(mesh):
    in_specs = (
        P(("grp", "seg"), None, None),
        P(("grp", "seg"), None, None),
        P(("grp", "seg"), None),
        P(None, "seg", None),
        P(None, "seg", None),
        P("grp", "seg", None),
        P("grp", "seg", None),
    )
    out_specs = (
        P(("grp", "seg"), None, None),
        P(("grp", "seg"), None, None),
        P("grp", "seg", None),
        P("grp", "seg", None),
        P("grp", "seg", None),
        P("grp", "seg", None),
    )
    return jax.shard_map(step, mesh=mesh, in_specs=in_specs, out_specs=out_specs, check_vma=False)
```
